32 devices in a mesh: tm: 8 (over y, x, core), lat: 4 (over z).
Axes of the slice: x: 2, y: 2, z: 4, core: 2. Of those that a mesh axis runs over, the one named last changes fastest.
Arguments:
- noisy_state: float32 [16, 8, 64, 1024], P(None, 'tm', None, 'lat'), may hold values from -6 to 6
- w_in: bfloat16 [128, 320], replicated, may hold values from -0.3125 to 0.3125
- w_mid: bfloat16 [128, 128], replicated, may hold values from -0.5 to 0.5
- w_out: bfloat16 [320, 128], replicated, may hold values from -0.5 to 0.5
- obs_pick: int32 [8, 4, 4, 2, 128], P('tm', 'lat'), may hold values from 0 to 16383, as said below
- obs_slot: int32 [8, 4, 4, 2], P('tm', 'lat'), may hold values from 0 to 7, as said below
- observed: float32 [8, 4, 1024], P('tm', 'lat'), may hold values from -6 to 6
- precision: bfloat16 [8, 4, 1024, 1024], P('tm', 'lat'), may hold values from -1 to 9, as said below
Outputs:
- updated: float32 [16, 8, 64, 1024], P(None, 'tm', None, 'lat')
The draws below stay inside these ranges and needn't reach their ends.
Inputs may be any that keep to these rules, and one draw needn't show every extreme that they name: `obs_pick`: within one time and band all entries are distinct; entry q names variable q // 256 at pixel q % 256 of that band. `obs_slot`: for each time, band and owner either all 2 entries are instrument positions or all equal 8 (nothing for that owner). For each time and owner, every position 0 to 7 appears exactly once over all bands, from exactly 4 bands. `precision`: Symmetric.
All inputs are finite; a program needn't handle non-finite values.
Results may differ from the reference program's by a relative error of at most 0.0053.
Values may be sent and summed in bfloat16 or wider, within the bound.
No kernel may reach another device: no remote copies, remote signals or barrier semaphores. Data moves between devices by JAX's collectives and lax.ppermute only.
A program may use at most 64 MiB of HBM per device.

```python
import math
import jax
import jax.numpy as jnp
from jax import lax

CHAN = 64
WIN = 5
HID = 128
MEMBERS = 16
PIX_DEV = 256
BLOCK = 128
INST_BLOCKS = 8
PAIR = 2
NT = 8
NPIX = 1024
INST = 1024
N_LAT = 4


def route_plan(key):
    base = jax.random.fold_in(key, 7)
    groups = INST_BLOCKS // PAIR

    def one_time(time_key):
        score_key, favour_key, order_key, pick_key = jax.random.split(time_key, 4)
        favour = jax.random.randint(favour_key, (N_LAT,), 0, 2) * 2 ** 19
        scores = (jax.random.randint(score_key, (N_LAT, N_LAT), 0, 2 ** 19) + favour[None, :]) * 64
        scores = scores + jnp.arange(N_LAT, dtype=jnp.int32)[None, :]
        chosen = lax.top_k(scores, groups)[1].astype(jnp.int32)
        orders = jax.vmap(lambda order_seed: jax.random.permutation(order_seed, INST_BLOCKS))(jax.random.split(order_key, N_LAT))
        orders = orders.astype(jnp.int32).reshape(N_LAT, groups, PAIR)
        matches = (chosen[:, :, None] == jnp.arange(N_LAT, dtype=jnp.int32)[None, None, :]).astype(jnp.int32)
        placed = jnp.sum(matches[:, :, :, None] * orders[:, :, None, :], axis=1)
        covered = jnp.sum(matches, axis=1)
        slot_table = placed + (1 - covered)[:, :, None] * INST_BLOCKS
        slot_table = jnp.transpose(slot_table, (1, 0, 2))
        chosen_cells = jax.vmap(lambda pick_seed: jax.random.permutation(pick_seed, CHAN * PIX_DEV)[:N_LAT * PAIR * BLOCK])(jax.random.split(pick_key, N_LAT))
        return (slot_table.astype(jnp.int32), chosen_cells.reshape(N_LAT, N_LAT, PAIR, BLOCK).astype(jnp.int32))
    return jax.vmap(one_time)(jax.random.split(base, NT))


def draw_obs_slot(key, part):
    return route_plan(key)[0]


def draw_obs_pick(key, part):
    return route_plan(key)[1]


def draw_precision(key, part):
    off_scale = 0.5 / math.sqrt(INST)

    def one_time(time_key):
        spread_key, diagonal_key = jax.random.split(time_key)
        spread_part = jax.random.normal(spread_key, (N_LAT, INST, INST), jnp.float32) * off_scale
        diagonal = jnp.exp(jax.random.uniform(diagonal_key, (N_LAT, INST), jnp.float32, 0.0, math.log(4.0)))
        symmetric = 0.5 * (spread_part + jnp.swapaxes(spread_part, 1, 2))
        whole = symmetric + diagonal[:, :, None] * jnp.eye(INST, dtype=jnp.float32)[None]
        return whole.astype(jnp.bfloat16)
    return lax.map(one_time, jax.random.split(jax.random.fold_in(key, 3), NT))


def levels(rng, dims, cuts, smallest, largest):
    def one(position, parts):
        heights = jax.random.uniform(jax.random.fold_in(jax.random.fold_in(rng, 6), position), (parts,), jnp.float32, smallest / len(cuts), largest / len(cuts))
        return jnp.repeat(jnp.exp(heights), dims[position] // parts).reshape((-1,) + (1,) * (len(dims) - position - 1))

    level = one(*cuts[0])
    for cut in cuts[1:]:
        level = level * one(*cut)
    return level


def scatter_about(rng, shape, scale, bound, shards=(), kind=jnp.bfloat16):
    drawn = scale * jax.random.normal(rng, shape, jnp.float32)
    if shards:
        drawn = drawn * levels(rng, shape, shards, -0.22, 0.18)
    return jnp.clip(drawn, -bound, bound).astype(kind)


def setup_inputs(seed: int = 0) -> dict:
    seeds = jax.random.split(jax.random.key(seed), 9)
    noisy_state = scatter_about(seeds[0], (MEMBERS, NT, CHAN, NPIX), 1.0, 6.0, ((1, 8), (3, 4)), jnp.float32)
    w_in = scatter_about(seeds[1], (HID, WIN * CHAN), (WIN * CHAN) ** -0.5, 0.3125)
    w_mid = scatter_about(seeds[2], (HID, HID), HID ** -0.5, 0.5)
    w_out = scatter_about(seeds[3], (WIN * CHAN, HID), HID ** -0.5, 0.5)
    obs_pick = draw_obs_pick(jax.random.fold_in(seeds[8], 71), 0)
    obs_slot = draw_obs_slot(jax.random.fold_in(seeds[8], 71), 0)
    observed = scatter_about(seeds[6], (NT, N_LAT, INST), 1.0, 6.0, ((0, 8), (1, 4)), jnp.float32)
    precision = draw_precision(jax.random.fold_in(seeds[8], 71), 0)
    return dict(noisy_state=noisy_state, w_in=w_in, w_mid=w_mid, w_out=w_out, obs_pick=obs_pick, obs_slot=obs_slot, observed=observed, precision=precision)


def silu_grad(values):
    sigma = jax.nn.sigmoid(values)
    return sigma * (1.0 + values * (1.0 - sigma))

def reference(noisy_state, w_in, w_mid, w_out, obs_pick, obs_slot, observed, precision):
    members, times, channels, pixels = noisy_state.shape
    radius = WIN // 2

    def product(form, weight, values):
        return jnp.einsum(form, weight.astype(jnp.float32), values.astype(jnp.float32), precision=lax.Precision.HIGHEST)

    def padded(values):
        return jnp.pad(values, ((0, 0), (radius, radius), (0, 0), (0, 0)))

    def window_at(source, start):
        return lax.dynamic_slice_in_dim(source, start, WIN, 1).reshape(members, WIN * channels, pixels)

    def activations(window):
        pre_one = product('hc,mcp->mhp', w_in, window)
        pre_two = product('gh,mhp->mgp', w_mid, jax.nn.silu(pre_one).astype(jnp.bfloat16))
        return (pre_one, pre_two)

    def intersection(totals, start, blocks):
        current = lax.dynamic_slice_in_dim(totals, start, WIN, 1)
        added = current + blocks.astype(jnp.float32).reshape(members, WIN, channels, pixels)
        return lax.dynamic_update_slice_in_dim(totals, added, start, 1)
    rounded = padded(noisy_state.astype(jnp.bfloat16))
    starts = jnp.arange(times, dtype=jnp.int32)
    zeroed = jnp.zeros((members, times + 2 * radius, channels, pixels), jnp.float32)

    def forward_step(totals, start):
        pre_one, pre_two = activations(window_at(rounded, start))
        blocks = product('ch,mhp->mcp', w_out, jax.nn.silu(pre_two).astype(jnp.bfloat16)).astype(jnp.bfloat16)
        return (intersection(totals, start, blocks), None)
    summed, _ = lax.scan(forward_step, zeroed, starts)
    denoised = noisy_state + summed[:, radius:radius + times]
    variable = obs_pick // PIX_DEV
    within = obs_pick % PIX_DEV
    band_ids = jnp.arange(N_LAT, dtype=jnp.int32)[None, :, None, None, None]
    global_index = (variable * NPIX + band_ids * PIX_DEV + within).astype(jnp.int32)
    flattened = denoised.reshape(members, times, channels * pixels)

    def take_cells(values, where):
        return jnp.take(values, where.reshape(-1), axis=1)
    predicted = jax.vmap(take_cells, in_axes=(1, 0), out_axes=1)(flattened, global_index)
    predicted = predicted.reshape(members, times, N_LAT, N_LAT, PAIR, BLOCK)
    selector = (obs_slot[..., None] == jnp.arange(INST_BLOCKS, dtype=jnp.int32)).astype(jnp.float32)
    gathered = jnp.einsum('tkors,mtkorb->mtosb', selector, predicted, precision=lax.Precision.HIGHEST)
    instrument = gathered.reshape(members, times, N_LAT, INST)
    innovation = (observed[None] - instrument).astype(jnp.bfloat16)

    def weigh(operands):
        matrices, vectors = operands
        return jnp.einsum('oij,moj->moi', matrices.astype(jnp.float32), vectors.astype(jnp.float32), precision=lax.Precision.HIGHEST)
    weighted = lax.map(weigh, (precision, jnp.transpose(innovation, (1, 0, 2, 3))))
    weighted = jnp.transpose(weighted, (1, 0, 2, 3)).reshape(members, times, N_LAT, INST_BLOCKS, BLOCK)
    returned = jnp.einsum('tkors,mtosb->mtkorb', selector, weighted, precision=lax.Precision.HIGHEST)

    def place_cells(values, where):
        return jnp.zeros((members, channels * pixels), jnp.float32).at[:, where.reshape(-1)].add(values.reshape(members, -1))
    guidance = jax.vmap(place_cells, in_axes=(1, 0), out_axes=1)(returned, global_index)
    guidance = guidance.reshape(members, times, channels, pixels)
    cotangent = padded(guidance.astype(jnp.bfloat16))

    def backward_step(totals, start):
        pre_one, pre_two = activations(window_at(rounded, start))
        incoming = window_at(cotangent, start)
        grad_two = (product('ch,mcp->mhp', w_out, incoming) * silu_grad(pre_two)).astype(jnp.bfloat16)
        grad_one = (product('gh,mgp->mhp', w_mid, grad_two) * silu_grad(pre_one)).astype(jnp.bfloat16)
        back_blocks = product('hc,mhp->mcp', w_in, grad_one).astype(jnp.bfloat16)
        return (intersection(totals, start, back_blocks), None)
    adjoint, _ = lax.scan(backward_step, zeroed, starts)
    return denoised + guidance + adjoint[:, radius:radius + times]
```

```python
import functools

import jax
import jax.numpy as jnp
from jax import lax
from jax.experimental import pallas as pl
from jax.experimental.pallas import tpu as pltpu
from jax.sharding import PartitionSpec as P

WIN = 5
LANES = 128
BF = jnp.bfloat16
F32 = jnp.float32


def ceil_to(value, step):
    return -(-value // step) * step


def silu_and_slope(values):
    sigma = 0.5 * jnp.tanh(0.5 * values) + 0.5
    silu = values * sigma
    return silu, sigma + silu - silu * sigma


def one_hot_rows(ref, time, base, block, count, dtype):
    width = ref.shape[2]
    per_row = width // LANES
    row = base + block // per_row
    start = (block % per_row) * LANES
    entry = ref[time, row : row + 1, start : start + LANES].astype(F32)
    index = lax.broadcasted_iota(jnp.int32, (count, LANES), 0).astype(F32)
    return index == entry


def forward_kernel(
    dims, offset_ref, recv_ref, win_ref, wmid_ref, wout_ref,
    send_ref, total_ref, slope_one_ref, slope_two_ref, padded, sums
):
    times, members, chan, width, owners, pairs, extra = dims
    radius = WIN // 2
    rows = members * chan
    blocks_obs = owners * pairs
    rows_each = blocks_obs * LANES // width
    zero_state = jnp.zeros((radius, members, chan, width), BF)
    padded[0:radius] = zero_state
    padded[radius + times :] = zero_state
    padded[radius : radius + times] = recv_ref[:, 0:rows, :].reshape(times, members, chan, width)
    sums[...] = jnp.zeros_like(sums)

    def window_step(s, carry):
        for m in range(members):
            window = padded[pl.ds(s, WIN), m].reshape(WIN * chan, width)
            pre_one = jnp.dot(win_ref[...], window, preferred_element_type=F32)
            hidden_one, slope_one = silu_and_slope(pre_one)
            pre_two = jnp.dot(wmid_ref[...], hidden_one.astype(BF), preferred_element_type=F32)
            hidden_two, slope_two = silu_and_slope(pre_two)
            blocks = jnp.dot(wout_ref[...], hidden_two.astype(BF), preferred_element_type=F32)
            sums[pl.ds(s, WIN), m] += blocks.reshape(WIN, chan, width)
            slope_one_ref[s, m] = slope_one.astype(slope_one_ref.dtype)
            slope_two_ref[s, m] = slope_two.astype(slope_two_ref.dtype)
        return carry

    lax.fori_loop(0, times, window_step, 0, unroll=times <= 8)
    offset = offset_ref[0]

    def gather_step(t, carry):
        field = sums[t + radius].reshape(rows, width)
        total_ref[t] = field
        state = (padded[t + radius].reshape(rows, width).astype(F32) + field).astype(BF)
        for o in range(owners):
            pieces = []
            for r in range(pairs):
                block = o * pairs + r
                place_row = rows + rows_each + block // (width // LANES)
                place_at = (block % (width // LANES)) * LANES
                place = recv_ref[t, place_row : place_row + 1, place_at : place_at + LANES].astype(F32)
                index = (lax.broadcasted_iota(jnp.int32, (width, LANES), 0) + offset).astype(F32)
                at_pixel = jnp.where(index == place, 1.0, 0.0).astype(BF)
                found = jnp.dot(state, at_pixel, preferred_element_type=F32)
                at_chan = one_hot_rows(recv_ref, t, rows, block, chan, F32)
                for m in range(members):
                    piece = found[m * chan : (m + 1) * chan]
                    pieces.append(jnp.sum(jnp.where(at_chan, piece, 0.0), axis=0, keepdims=True))
            for r in range(pairs):
                block = o * pairs + r
                slot_row = rows + 2 * rows_each + block // (width // LANES)
                slot_at = (block % (width // LANES)) * LANES
                pieces.append(recv_ref[t, slot_row : slot_row + 1, slot_at : slot_at + LANES].astype(F32))
            spare = send_ref.shape[1] - len(pieces)
            if spare:
                pieces.append(jnp.zeros((spare, LANES), F32))
            send_ref[t * owners + o] = jnp.concatenate(pieces, axis=0).astype(BF)
        return carry

    lax.fori_loop(0, times, gather_step, 0, unroll=times <= 8)


def owner_kernel(dims, recv_ref, observed_ref, precision_ref, send_ref, arrived, slots):
    groups, parts, members, bands, pairs, positions = dims
    for b in range(bands):
        for g in range(groups):
            tile = recv_ref[(g * parts) * bands + b].astype(F32)
            for part in range(1, parts):
                other = recv_ref[(g * parts + part) * bands + b].astype(F32)
                tile = tile + other
            for r in range(pairs):
                arrived[b * pairs + r, g * members : (g + 1) * members] = tile[r * members : (r + 1) * members]
        first = recv_ref[b].astype(F32)
        for r in range(pairs):
            row = pairs * members + r
            slots[b * pairs + r] = jnp.broadcast_to(first[row : row + 1], slots.shape[1:])
    innovation = []
    for n in range(positions):
        vector = jnp.zeros(arrived.shape[1:], F32)
        for k in range(bands * pairs):
            vector = vector + jnp.where(slots[k] == float(n), arrived[k], 0.0)
        innovation.append((observed_ref[n : n + 1] - vector).astype(BF))
    innovation = jnp.concatenate(innovation, axis=1)
    weighted = jnp.dot(innovation, precision_ref[...], preferred_element_type=F32)
    for b in range(bands):
        answers = []
        for r in range(pairs):
            slot = slots[b * pairs + r]
            answer = jnp.zeros(arrived.shape[1:], F32)
            for n in range(positions):
                answer = answer + jnp.where(slot == float(n), weighted[:, n * LANES : (n + 1) * LANES], 0.0)
            answers.append(answer)
        for g in range(groups):
            pieces = [answer[g * members : (g + 1) * members] for answer in answers]
            spare = send_ref.shape[1] - pairs * members
            if spare:
                pieces.append(jnp.zeros((spare, LANES), F32))
            tile = jnp.concatenate(pieces, axis=0).astype(BF)
            for part in range(parts):
                send_ref[(g * parts + part) * bands + b] = tile


def backward_kernel(
    dims, offset_ref, recv_ref, picks_ref, win_ref, wmid_ref, wout_ref, total_ref, slope_one_ref, slope_two_ref,
    out_ref, padded, sums
):
    times, members, chan, width, owners, pairs, extra = dims
    radius = WIN // 2
    rows = members * chan
    blocks_obs = owners * pairs
    rows_each = blocks_obs * LANES // width
    per_row = width // LANES
    zero_state = jnp.zeros((radius, members, chan, width), BF)
    padded[0:radius] = zero_state
    padded[radius + times :] = zero_state
    sums[0:radius] = jnp.zeros((radius, members, chan, width), F32)
    sums[radius + times :] = jnp.zeros((radius, members, chan, width), F32)
    offset = offset_ref[0]

    def scatter_step(t, carry):
        guidance = jnp.zeros((rows, width), F32)
        for o in range(owners):
            tile = recv_ref[t * owners + o].astype(F32)
            for r in range(pairs):
                block = o * pairs + r
                at = (block % per_row) * LANES
                chan_row = rows + block // per_row
                place_row = chan_row + rows_each
                place = picks_ref[t, place_row : place_row + 1, at : at + LANES].astype(F32)
                index = (lax.broadcasted_iota(jnp.int32, (width, LANES), 0) + offset).astype(F32)
                at_pixel = jnp.where(index == place, 1.0, 0.0).astype(BF)
                where_chan = picks_ref[t, chan_row : chan_row + 1, at : at + LANES].astype(F32)
                at_chan = lax.broadcasted_iota(jnp.int32, (chan, LANES), 0).astype(F32) == where_chan
                spread = []
                for m in range(members):
                    row = r * members + m
                    spread.append(jnp.where(at_chan, tile[row : row + 1], 0.0))
                spread = jnp.concatenate(spread, axis=0).astype(BF)
                guidance = guidance + lax.dot_general(
                    spread, at_pixel, (((1,), (1,)), ((), ())), preferred_element_type=F32
                )
        padded[t + radius] = guidance.astype(BF).reshape(members, chan, width)
        sums[t + radius] = (guidance + total_ref[t]).reshape(members, chan, width)
        return carry

    lax.fori_loop(0, times, scatter_step, 0, unroll=times <= 8)
    turned = (((0,), (0,)), ((), ()))

    def window_step(s, carry):
        for m in range(members):
            window = padded[pl.ds(s, WIN), m].reshape(WIN * chan, width)
            grad_two = lax.dot_general(wout_ref[...], window, turned, preferred_element_type=F32)
            grad_two = (grad_two * slope_two_ref[s, m].astype(F32)).astype(BF)
            grad_one = lax.dot_general(wmid_ref[...], grad_two, turned, preferred_element_type=F32)
            grad_one = (grad_one * slope_one_ref[s, m].astype(F32)).astype(BF)
            blocks = lax.dot_general(win_ref[...], grad_one, turned, preferred_element_type=F32)
            sums[pl.ds(s, WIN), m] += blocks.reshape(WIN, chan, width)
        return carry

    lax.fori_loop(0, times, window_step, 0, unroll=times <= 8)
    for t in range(times):
        out_ref[t] = sums[t + radius].reshape(rows, width).astype(BF)


def body(noisy_state, w_in, w_mid, w_out, obs_pick, obs_slot, observed, precision):
    current = noisy_state[:, 0]
    all_members, chan, pixels = current.shape
    times = lax.axis_size("tm")
    bands = lax.axis_size("lat")
    owners, pairs, block_rows = obs_pick.shape[2:]
    positions = observed.shape[2] // block_rows
    parts = max(1, times // all_members)
    groups = times // parts
    members = all_members // groups
    width = pixels // parts
    radius = WIN // 2
    rows = members * chan
    hidden = w_mid.shape[0]
    pick = obs_pick[0, 0].reshape(-1)
    slot = jnp.broadcast_to(obs_slot[0, 0][:, :, None], (owners, pairs, block_rows)).reshape(-1)
    extras = jnp.stack([pick // pixels, pick % pixels, slot]).astype(BF)
    rows_each = extras.shape[1] // width
    extra = ceil_to(3 * rows_each, 16)
    extras = extras.reshape(3 * rows_each, width)
    extras = jnp.pad(extras, ((0, extra - 3 * rows_each), (0, 0)))
    state = current.astype(BF).reshape(groups, rows, parts, width)
    state = state.transpose(0, 2, 1, 3).reshape(times, rows, width)
    payload = jnp.concatenate([state, jnp.broadcast_to(extras[None], (times, extra, width))], axis=1)
    received = lax.all_to_all(payload, "tm", split_axis=0, concat_axis=0, tiled=True)

    offset = ((lax.axis_index("tm") % parts) * width).astype(jnp.int32).reshape(1)
    dims = (times, members, chan, width, owners, pairs, extra)
    smem = pl.BlockSpec(memory_space=pltpu.SMEM)
    vmem = pl.BlockSpec(memory_space=pltpu.VMEM)
    rows_two = ceil_to(members * pairs + pairs, 8)
    packed, total, slope_one, slope_two = pl.pallas_call(
        functools.partial(forward_kernel, dims),
        out_shape=(
            jax.ShapeDtypeStruct((times * owners, rows_two, LANES), BF),
            jax.ShapeDtypeStruct((times, rows, width), F32),
            jax.ShapeDtypeStruct((times, members, hidden, width), F32),
            jax.ShapeDtypeStruct((times, members, hidden, width), F32),
        ),
        in_specs=[smem, vmem, vmem, vmem, vmem],
        out_specs=(vmem,) * 4,
        scratch_shapes=[
            pltpu.VMEM((times + 2 * radius, members, chan, width), BF),
            pltpu.VMEM((times + 2 * radius, members, chan, width), F32),
        ],
        name="forward",
    )(offset, received, w_in, w_mid, w_out)
    arrived = lax.all_to_all(packed, ("tm", "lat"), split_axis=0, concat_axis=0, tiled=True)
    rows_three = ceil_to(members * pairs, 2)
    answer = pl.pallas_call(
        functools.partial(owner_kernel, (groups, parts, members, bands, pairs, positions)),
        out_shape=jax.ShapeDtypeStruct((times * bands, rows_three, LANES), BF),
        in_specs=[vmem, vmem, vmem],
        out_specs=vmem,
        scratch_shapes=[
            pltpu.VMEM((bands * pairs, all_members, LANES), F32),
            pltpu.VMEM((bands * pairs, all_members, LANES), F32),
        ],
        name="owner",
    )(arrived, observed.reshape(positions, block_rows), precision[0, 0])
    returned = lax.all_to_all(answer, ("tm", "lat"), split_axis=0, concat_axis=0, tiled=True)
    change = pl.pallas_call(
        functools.partial(backward_kernel, dims),
        out_shape=jax.ShapeDtypeStruct((times, rows, width), BF),
        in_specs=[smem] + [vmem] * 8,
        out_specs=vmem,
        scratch_shapes=[
            pltpu.VMEM((times + 2 * radius, members, chan, width), BF),
            pltpu.VMEM((times + 2 * radius, members, chan, width), F32),
        ],
        name="backward",
    )(offset, returned, received, w_in, w_mid, w_out, total, slope_one, slope_two)
    back = lax.all_to_all(change, "tm", split_axis=0, concat_axis=0, tiled=True)
    back = back.reshape(groups, parts, members, chan, width).transpose(0, 2, 3, 1, 4)
    updated = current + back.reshape(all_members, chan, pixels).astype(F32)
    return updated[:, None]


def solution(mesh):
    in_specs = (
        P(None, "tm", None, "lat"),
        P(),
        P(),
        P(),
        P("tm", "lat", None, None, None),
        P("tm", "lat", None, None),
        P("tm", "lat", None),
        P("tm", "lat", None, None),
    )
    out_specs = P(None, "tm", None, "lat")
    return jax.shard_map(body, mesh=mesh, in_specs=in_specs, out_specs=out_specs, check_vma=False)
```

```python
import functools

import jax
import jax.numpy as jnp
from jax import lax
from jax.experimental import pallas as pl
from jax.experimental.pallas import tpu as pltpu
from jax.sharding import PartitionSpec as P

WIN = 5
LANES = 128
BF = jnp.bfloat16
F32 = jnp.float32


def limit(mib):
    return pltpu.CompilerParams(vmem_limit_bytes=mib * 2**20)


def ceil_to(value, step):
    return -(-value // step) * step


def silu(values):
    half = 0.5 * values
    return half + half * jnp.tanh(half)


def silu_slope(values):
    half = 0.5 * values
    bend = jnp.tanh(half)
    return (0.5 + 0.5 * bend) * (1.0 + half * (1.0 - bend))


def loop(count, step):
    if count <= 8:
        for index in range(count):
            step(index)
    else:
        lax.fori_loop(0, count, lambda index, carry: (step(index), carry)[1], 0)


def pack_kernel(
    dims, state_hbm, pick_hbm, slot_hbm, win_turned_hbm, wmid_hbm, wout_hbm,
    out, win_ref, wmid_turned_ref, wout_turned_ref,
    state, pick_vmem, slot_ref, win_turned, wmid, wout, state_sems, sems
):
    groups, parts, members, chan, width, owners, pairs, extra = dims
    rows = members * chan
    per_row = width // LANES
    rows_each = owners * pairs // per_row
    chunks = state_sems.shape[0]
    step = groups // chunks
    small = []
    pairs_of = ((pick_hbm, pick_vmem), (slot_hbm, slot_ref), (win_turned_hbm, win_turned), (wmid_hbm, wmid), (wout_hbm, wout))
    for index, (source, target) in enumerate(pairs_of[:2]):
        small.append(pltpu.make_async_copy(source, target, sems.at[index]))
        small[-1].start()
    copies = []
    for c in range(chunks):
        span = pl.ds(c * step * members, step * members)
        copies.append(pltpu.make_async_copy(state_hbm.at[span], state.at[span], state_sems.at[c]))
        copies[-1].start()
    for index, (source, target) in enumerate(pairs_of):
        if index >= 2:
            small.append(pltpu.make_async_copy(source, target, sems.at[index]))
            small[-1].start()
    small[0].wait()
    small[1].wait()
    pick = pick_vmem[...].astype(F32)
    channel = jnp.floor((pick + 0.5) * (1.0 / (width * parts)))
    place = pick - channel * (width * parts)
    lines = []
    for values in (channel, place):
        for row in range(rows_each):
            cells = [divmod(row * per_row + k, pairs) for k in range(per_row)]
            lines.append(jnp.concatenate([values[o, r : r + 1] for o, r in cells], axis=1))
    for row in range(rows_each):
        cells = [divmod(row * per_row + k, pairs) for k in range(per_row)]
        lines.append(jnp.concatenate([jnp.full((1, LANES), slot_ref[r, o].astype(F32)) for o, r in cells], axis=1))
    if extra > len(lines):
        lines.append(jnp.zeros((extra - len(lines), width), F32))
    lines = jnp.concatenate(lines, axis=0).astype(BF)
    for d in range(groups * parts):
        out[d, rows:] = lines
    for c in range(chunks):
        copies[c].wait()
        for g in range(c * step, (c + 1) * step):
            block = state[g * members : (g + 1) * members].astype(BF)
            for part in range(parts):
                piece = block[:, :, part * width : (part + 1) * width]
                out[g * parts + part, 0:rows] = piece.reshape(rows, width)
    for copy in small[2:]:
        copy.wait()
    win_ref[...] = win_turned[...].T
    wmid_turned_ref[...] = wmid[...].T
    wout_turned_ref[...] = wout[...].T


def row_of(ref, time, base, block):
    per_row = ref.shape[2] // LANES
    row = base + block // per_row
    start = (block % per_row) * LANES
    return ref[time, row : row + 1, start : start + LANES].astype(F32)


def forward_kernel(
    dims, offset_ref, recv_ref, win_ref, wmid_ref, wout_ref,
    send_ref, total_ref, pre_one_ref, pre_two_ref, at_pixel_ref, padded, sums, hidden_one, hidden_two
):
    times, members, chan, width, owners, pairs, extra = dims
    radius = WIN // 2
    rows = members * chan
    rows_each = owners * pairs * LANES // width
    zero_state = jnp.zeros((radius, members, chan, width), BF)
    padded[0:radius] = zero_state
    padded[radius + times :] = zero_state
    padded[radius : radius + times] = recv_ref[:, 0:rows, :].reshape(times, members, chan, width)
    sums[...] = jnp.zeros_like(sums)

    def first(s):
        for m in range(members):
            window = padded[pl.ds(s, WIN), m].reshape(WIN * chan, width)
            pre_one = jnp.dot(win_ref[...], window, preferred_element_type=F32)
            pre_one_ref[s, m] = pre_one
            hidden_one[s, m] = silu(pre_one).astype(BF)

    def second(s):
        for m in range(members):
            pre_two = jnp.dot(wmid_ref[...], hidden_one[s, m], preferred_element_type=F32)
            pre_two_ref[s, m] = pre_two
            hidden_two[s, m] = silu(pre_two).astype(BF)

    def third(s):
        for m in range(members):
            blocks = jnp.dot(wout_ref[...], hidden_two[s, m], preferred_element_type=F32)
            sums[pl.ds(s, WIN), m] += blocks.reshape(WIN, chan, width)

    offset = offset_ref[0]
    eight = 8

    def gather(t):
        field = sums[t + radius]
        total_ref[t] = field.reshape(rows, width)
        state = (padded[t + radius].astype(F32) + field).astype(BF).reshape(rows, width)
        index = (lax.broadcasted_iota(jnp.int32, (width, LANES), 0) + offset).astype(F32)
        for o in range(owners):
            lines = []
            for r in range(pairs):
                place = row_of(recv_ref, t, rows + rows_each, o * pairs + r)
                lines.append(jnp.where(index == place, 1.0, 0.0).astype(BF))
            at_pixel = jnp.concatenate(lines, axis=1)
            at_pixel_ref[t, :, o * pairs * LANES : (o + 1) * pairs * LANES] = at_pixel
            found = jnp.dot(state, at_pixel, preferred_element_type=F32)
            pieces = []
            for r in range(pairs):
                channel = row_of(recv_ref, t, rows, o * pairs + r)
                high = jnp.floor(channel * (1.0 / eight))
                at_row = lax.broadcasted_iota(jnp.int32, (eight, LANES), 0).astype(F32) == channel - high * eight
                high = jnp.broadcast_to(high, (eight, LANES))
                span = slice(r * LANES, (r + 1) * LANES)
                picked = [found[m * chan : m * chan + eight, span] for m in range(members)]
                for c in range(1, chan // eight):
                    here = high == float(c)
                    for m in range(members):
                        start = m * chan + c * eight
                        picked[m] = jnp.where(here, found[start : start + eight, span], picked[m])
                for m in range(members):
                    pieces.append(jnp.sum(jnp.where(at_row, picked[m], 0.0), axis=0, keepdims=True))
            for r in range(pairs):
                pieces.append(row_of(recv_ref, t, rows + 2 * rows_each, o * pairs + r))
            spare = send_ref.shape[1] - len(pieces)
            if spare:
                pieces.append(jnp.zeros((spare, LANES), F32))
            send_ref[t * owners + o] = jnp.concatenate(pieces, axis=0).astype(BF)

    loop(times, first)
    loop(times, second)
    loop(times, third)
    loop(times, gather)


def owner_kernel(dims, recv_ref, observed_ref, precision_ref, send_ref, arrived, slots):
    groups, parts, members, bands, pairs, positions = dims
    for b in range(bands):
        for g in range(groups):
            tile = recv_ref[(g * parts) * bands + b].astype(F32)
            for part in range(1, parts):
                other = recv_ref[(g * parts + part) * bands + b].astype(F32)
                tile = tile + other
            for r in range(pairs):
                arrived[b * pairs + r, g * members : (g + 1) * members] = tile[r * members : (r + 1) * members]
        first = recv_ref[b].astype(F32)
        for r in range(pairs):
            row = pairs * members + r
            slots[b * pairs + r] = jnp.broadcast_to(first[row : row + 1], slots.shape[1:])
    innovation = []
    for n in range(positions):
        vector = jnp.zeros(arrived.shape[1:], F32)
        for k in range(bands * pairs):
            vector = vector + jnp.where(slots[k] == float(n), arrived[k], 0.0)
        innovation.append((observed_ref[n : n + 1] - vector).astype(BF))
    innovation = jnp.concatenate(innovation, axis=1)
    weighted = jnp.dot(innovation, precision_ref[...], preferred_element_type=F32)
    for b in range(bands):
        answers = []
        for r in range(pairs):
            slot = slots[b * pairs + r]
            answer = jnp.zeros(arrived.shape[1:], F32)
            for n in range(positions):
                answer = answer + jnp.where(slot == float(n), weighted[:, n * LANES : (n + 1) * LANES], 0.0)
            answers.append(answer)
        for g in range(groups):
            pieces = [answer[g * members : (g + 1) * members] for answer in answers]
            spare = send_ref.shape[1] - pairs * members
            if spare:
                pieces.append(jnp.zeros((spare, LANES), F32))
            tile = jnp.concatenate(pieces, axis=0).astype(BF)
            for part in range(parts):
                send_ref[(g * parts + part) * bands + b] = tile


def backward_kernel(
    dims, recv_ref, picks_ref, at_pixel_ref, win_ref, wmid_ref, wout_ref, total_ref, pre_one_ref, pre_two_ref,
    out_ref, padded, sums, grad_one, grad_two
):
    times, members, chan, width, owners, pairs, extra = dims
    radius = WIN // 2
    rows = members * chan
    zero_state = jnp.zeros((radius, members, chan, width), BF)
    padded[0:radius] = zero_state
    padded[radius + times :] = zero_state
    sums[0:radius] = jnp.zeros((radius, members, chan, width), F32)
    sums[radius + times :] = jnp.zeros((radius, members, chan, width), F32)

    def scatter(t):
        spread = []
        index = lax.broadcasted_iota(jnp.int32, (chan, LANES), 0).astype(F32)
        for o in range(owners):
            tile = recv_ref[t * owners + o].astype(F32)
            for r in range(pairs):
                at_chan = index == row_of(picks_ref, t, rows, o * pairs + r)
                pieces = []
                for m in range(members):
                    row = r * members + m
                    pieces.append(jnp.where(at_chan, tile[row : row + 1], 0.0).astype(BF))
                spread.append(jnp.concatenate(pieces, axis=0))
        spread = jnp.concatenate(spread, axis=1)
        guidance = lax.dot_general(
            spread, at_pixel_ref[t], (((1,), (1,)), ((), ())), preferred_element_type=F32
        )
        padded[t + radius] = guidance.astype(BF).reshape(members, chan, width)
        sums[t + radius] = (guidance + total_ref[t]).reshape(members, chan, width)

    def first(s):
        for m in range(members):
            window = padded[pl.ds(s, WIN), m].reshape(WIN * chan, width)
            grad = jnp.dot(wout_ref[...], window, preferred_element_type=F32)
            grad_two[s, m] = (grad * silu_slope(pre_two_ref[s, m])).astype(BF)

    def second(s):
        for m in range(members):
            grad = jnp.dot(wmid_ref[...], grad_two[s, m], preferred_element_type=F32)
            grad_one[s, m] = (grad * silu_slope(pre_one_ref[s, m])).astype(BF)

    def third(s):
        for m in range(members):
            blocks = jnp.dot(win_ref[...], grad_one[s, m], preferred_element_type=F32)
            sums[pl.ds(s, WIN), m] += blocks.reshape(WIN, chan, width)

    loop(times, scatter)
    loop(times, first)
    loop(times, second)
    loop(times, third)

    def finish(t):
        out_ref[t] = sums[t + radius].reshape(rows, width).astype(BF)

    loop(times, finish)


def body(noisy_state, w_in, w_mid, w_out, obs_pick, obs_slot, observed, precision):
    current = noisy_state[:, 0]
    all_members, chan, pixels = current.shape
    times = lax.axis_size("tm")
    bands = lax.axis_size("lat")
    owners, pairs, block_rows = obs_pick.shape[2:]
    positions = observed.shape[2] // block_rows
    parts = max(1, times // all_members)
    groups = times // parts
    members = all_members // groups
    width = pixels // parts
    radius = WIN // 2
    rows = members * chan
    hidden = w_mid.shape[0]
    extra = ceil_to(3 * owners * pairs * block_rows // width, 16)
    smem = pl.BlockSpec(memory_space=pltpu.SMEM)
    vmem = pl.BlockSpec(memory_space=pltpu.VMEM)
    hbm = pl.BlockSpec(memory_space=pltpu.HBM)
    chunks = 4 if groups % 4 == 0 else 1
    payload, win, wmid_turned, wout_turned = pl.pallas_call(
        functools.partial(pack_kernel, (groups, parts, members, chan, width, owners, pairs, extra)),
        out_shape=(
            jax.ShapeDtypeStruct((times, rows + extra, width), BF),
            jax.ShapeDtypeStruct(w_in.shape, BF),
            jax.ShapeDtypeStruct(w_mid.shape[::-1], BF),
            jax.ShapeDtypeStruct(w_out.shape[::-1], BF),
        ),
        in_specs=[hbm] * 6,
        out_specs=(vmem,) * 4,
        scratch_shapes=[
            pltpu.VMEM(current.shape, F32),
            pltpu.VMEM((owners, pairs, block_rows), jnp.int32),
            pltpu.SMEM((pairs, owners), jnp.int32),
            pltpu.VMEM(w_in.shape[::-1], BF),
            pltpu.VMEM(w_mid.shape, BF),
            pltpu.VMEM(w_out.shape, BF),
            pltpu.SemaphoreType.DMA((chunks,)),
            pltpu.SemaphoreType.DMA((5,)),
        ],
        compiler_params=limit(16),
        name="pack",
    )(*(pltpu.with_memory_space_constraint(x, pltpu.HBM) for x in (current, obs_pick[0, 0], obs_slot[0, 0].T, w_in.T, w_mid, w_out)))
    received = lax.all_to_all(payload, "tm", split_axis=0, concat_axis=0, tiled=True)

    offset = ((lax.axis_index("tm") % parts) * width).astype(jnp.int32).reshape(1)
    dims = (times, members, chan, width, owners, pairs, extra)
    rows_two = ceil_to(members * pairs + pairs, 8)
    inner = (times, members, hidden, width)
    padded_shape = (times + 2 * radius, members, chan, width)
    packed, total, pre_one, pre_two, at_pixel = pl.pallas_call(
        functools.partial(forward_kernel, dims),
        out_shape=(
            jax.ShapeDtypeStruct((times * owners, rows_two, LANES), BF),
            jax.ShapeDtypeStruct((times, rows, width), F32),
            jax.ShapeDtypeStruct(inner, F32),
            jax.ShapeDtypeStruct(inner, F32),
            jax.ShapeDtypeStruct((times, width, owners * pairs * block_rows), BF),
        ),
        in_specs=[smem, vmem, vmem, vmem, vmem],
        out_specs=(vmem,) * 5,
        scratch_shapes=[
            pltpu.VMEM(padded_shape, BF),
            pltpu.VMEM(padded_shape, F32),
            pltpu.VMEM(inner, BF),
            pltpu.VMEM(inner, BF),
        ],
        compiler_params=limit(24),
        name="forward",
    )(offset, received, win, w_mid, w_out)
    arrived = lax.all_to_all(packed, ("tm", "lat"), split_axis=0, concat_axis=0, tiled=True)
    rows_three = ceil_to(members * pairs, 2)
    answer = pl.pallas_call(
        functools.partial(owner_kernel, (groups, parts, members, bands, pairs, positions)),
        out_shape=jax.ShapeDtypeStruct((times * bands, rows_three, LANES), BF),
        in_specs=[vmem, vmem, vmem],
        out_specs=vmem,
        scratch_shapes=[
            pltpu.VMEM((bands * pairs, all_members, LANES), F32),
            pltpu.VMEM((bands * pairs, all_members, LANES), F32),
        ],
        compiler_params=limit(16),
        name="owner",
    )(arrived, observed.reshape(positions, block_rows), precision[0, 0])
    returned = lax.all_to_all(answer, ("tm", "lat"), split_axis=0, concat_axis=0, tiled=True)
    change = pl.pallas_call(
        functools.partial(backward_kernel, dims),
        out_shape=jax.ShapeDtypeStruct((times, rows, width), BF),
        in_specs=[vmem] * 9,
        out_specs=vmem,
        scratch_shapes=[
            pltpu.VMEM(padded_shape, BF),
            pltpu.VMEM(padded_shape, F32),
            pltpu.VMEM(inner, BF),
            pltpu.VMEM(inner, BF),
        ],
        compiler_params=limit(24),
        name="backward",
    )(returned, received, at_pixel, w_in.T, wmid_turned, wout_turned, total, pre_one, pre_two)
    back = lax.all_to_all(change, "tm", split_axis=0, concat_axis=0, tiled=True)
    back = back.reshape(groups, parts, members, chan, width).transpose(0, 2, 3, 1, 4)
    updated = current + back.reshape(all_members, chan, pixels).astype(F32)
    return updated[:, None]


def solution(mesh):
    in_specs = (
        P(None, "tm", None, "lat"),
        P(),
        P(),
        P(),
        P("tm", "lat", None, None, None),
        P("tm", "lat", None, None),
        P("tm", "lat", None),
        P("tm", "lat", None, None),
    )
    out_specs = P(None, "tm", None, "lat")
    return jax.shard_map(body, mesh=mesh, in_specs=in_specs, out_specs=out_specs, check_vma=False)
```

```python
import functools

import jax
import jax.numpy as jnp
from jax import lax
from jax.experimental import pallas as pl
from jax.experimental.pallas import tpu as pltpu
from jax.sharding import PartitionSpec as P

WIN = 5
LANES = 128
BF = jnp.bfloat16
F32 = jnp.float32


def limit(mib):
    return pltpu.CompilerParams(vmem_limit_bytes=mib * 2**20)


def ceil_to(value, step):
    return -(-value // step) * step


def silu_of_half(half):
    return half + half * jnp.tanh(half)


def twice_slope_of_half(half):
    bend = jnp.tanh(half)
    return (1.0 + bend) * (1.0 + half * (1.0 - bend))


def loop(count, step):
    if count <= 8:
        for index in range(count):
            step(index)
    else:
        lax.fori_loop(0, count, lambda index, carry: (step(index), carry)[1], 0)


def pack_kernel(
    dims, state_hbm, pick_hbm, slot_hbm, win_turned_hbm, wmid_hbm, wout_hbm,
    out, win_ref, wmid_ref, wmid_turned_ref, wout_turned_ref,
    state, pick_vmem, slot_ref, win_turned, wmid, wout, state_sems, sems
):
    groups, parts, members, chan, width, owners, pairs, extra = dims
    rows = members * chan
    per_row = width // LANES
    rows_each = owners * pairs // per_row
    chunks = state_sems.shape[0]
    step = groups // chunks
    small = []
    pairs_of = ((pick_hbm, pick_vmem), (slot_hbm, slot_ref), (win_turned_hbm, win_turned), (wmid_hbm, wmid), (wout_hbm, wout))
    for index, (source, target) in enumerate(pairs_of[:2]):
        small.append(pltpu.make_async_copy(source, target, sems.at[index]))
        small[-1].start()
    copies = []
    for c in range(chunks):
        span = pl.ds(c * step * members, step * members)
        copies.append(pltpu.make_async_copy(state_hbm.at[span], state.at[span], state_sems.at[c]))
        copies[-1].start()
    for index, (source, target) in enumerate(pairs_of):
        if index >= 2:
            small.append(pltpu.make_async_copy(source, target, sems.at[index]))
            small[-1].start()
    small[0].wait()
    small[1].wait()
    pick = pick_vmem[...].astype(F32)
    channel = jnp.floor((pick + 0.5) * (1.0 / (width * parts)))
    place = pick - channel * (width * parts)
    lines = []
    for values in (channel, place):
        for row in range(rows_each):
            cells = [divmod(row * per_row + k, pairs) for k in range(per_row)]
            lines.append(jnp.concatenate([values[o, r : r + 1] for o, r in cells], axis=1))
    for row in range(rows_each):
        cells = [divmod(row * per_row + k, pairs) for k in range(per_row)]
        lines.append(jnp.concatenate([jnp.full((1, LANES), slot_ref[r, o].astype(F32)) for o, r in cells], axis=1))
    if extra > len(lines):
        lines.append(jnp.zeros((extra - len(lines), width), F32))
    lines = jnp.concatenate(lines, axis=0).astype(BF)
    for d in range(groups * parts):
        out[d, rows:] = lines
    for c in range(chunks):
        copies[c].wait()
        for g in range(c * step, (c + 1) * step):
            block = state[g * members : (g + 1) * members].astype(BF)
            for part in range(parts):
                piece = block[:, :, part * width : (part + 1) * width]
                out[g * parts + part, 0:rows] = piece.reshape(rows, width)
    for copy in small[2:]:
        copy.wait()
    half = jnp.asarray(0.5, BF)
    win_ref[...] = win_turned[...].T * half
    wmid_ref[...] = wmid[...] * half
    wmid_turned_ref[...] = wmid[...].T * half
    wout_turned_ref[...] = wout[...].T * half


def row_of(ref, time, base, block):
    per_row = ref.shape[2] // LANES
    row = base + block // per_row
    start = (block % per_row) * LANES
    return ref[time, row : row + 1, start : start + LANES].astype(F32)


def forward_kernel(
    dims, offset_ref, recv_ref, win_ref, wmid_ref, wout_ref,
    send_ref, total_ref, pre_one_ref, pre_two_ref, at_pixel_ref, padded, sums, hidden_one, hidden_two
):
    times, members, chan, width, owners, pairs, extra = dims
    radius = WIN // 2
    rows = members * chan
    rows_each = owners * pairs * LANES // width
    zero_state = jnp.zeros((radius, members, chan, width), BF)
    padded[0:radius] = zero_state
    padded[radius + times :] = zero_state
    padded[radius : radius + times] = recv_ref[:, 0:rows, :].reshape(times, members, chan, width)
    sums[...] = jnp.zeros_like(sums)

    def first(s):
        for m in range(members):
            window = padded[pl.ds(s, WIN), m].reshape(WIN * chan, width)
            pre_one = jnp.dot(win_ref[...], window, preferred_element_type=F32)
            pre_one_ref[s, m] = pre_one
            hidden_one[s, m] = silu_of_half(pre_one).astype(BF)

    def second(s):
        for m in range(members):
            pre_two = jnp.dot(wmid_ref[...], hidden_one[s, m], preferred_element_type=F32)
            pre_two_ref[s, m] = pre_two
            hidden_two[s, m] = silu_of_half(pre_two).astype(BF)

    def third(s):
        for m in range(members):
            blocks = jnp.dot(wout_ref[...], hidden_two[s, m], preferred_element_type=F32)
            sums[pl.ds(s, WIN), m] += blocks.reshape(WIN, chan, width)

    offset = offset_ref[0]
    eight = 8

    def gather(t):
        field = sums[t + radius]
        total_ref[t] = field.reshape(rows, width)
        state = (padded[t + radius].astype(F32) + field).astype(BF).reshape(rows, width)
        index = (lax.broadcasted_iota(jnp.int32, (width, LANES), 0) + offset).astype(BF)
        for o in range(owners):
            lines = []
            for r in range(pairs):
                place = row_of(recv_ref, t, rows + rows_each, o * pairs + r)
                here = index == place.astype(BF)
                lines.append(jnp.where(here, jnp.ones_like(index), jnp.zeros_like(index)))
            at_pixel = jnp.concatenate(lines, axis=1)
            at_pixel_ref[t, o * pairs * LANES : (o + 1) * pairs * LANES] = at_pixel.T
            found = jnp.dot(state, at_pixel, preferred_element_type=F32)
            pieces = []
            for r in range(pairs):
                channel = row_of(recv_ref, t, rows, o * pairs + r)
                high = jnp.floor(channel * (1.0 / eight))
                at_row = lax.broadcasted_iota(jnp.int32, (eight, LANES), 0).astype(F32) == channel - high * eight
                high = jnp.broadcast_to(high, (eight, LANES))
                span = slice(r * LANES, (r + 1) * LANES)
                picked = [found[m * chan : m * chan + eight, span] for m in range(members)]
                for c in range(1, chan // eight):
                    here = high == float(c)
                    for m in range(members):
                        start = m * chan + c * eight
                        picked[m] = jnp.where(here, found[start : start + eight, span], picked[m])
                for m in range(members):
                    pieces.append(jnp.sum(jnp.where(at_row, picked[m], 0.0), axis=0, keepdims=True))
            for r in range(pairs):
                pieces.append(row_of(recv_ref, t, rows + 2 * rows_each, o * pairs + r))
            spare = send_ref.shape[1] - len(pieces)
            if spare:
                pieces.append(jnp.zeros((spare, LANES), F32))
            send_ref[t * owners + o] = jnp.concatenate(pieces, axis=0).astype(BF)

    loop(times, first)
    loop(times, second)
    loop(times, third)
    loop(times, gather)


def owner_kernel(dims, recv_ref, observed_ref, precision_ref, send_ref, arrived, slots):
    groups, parts, members, bands, pairs, positions = dims
    for b in range(bands):
        for g in range(groups):
            tile = recv_ref[(g * parts) * bands + b].astype(F32)
            for part in range(1, parts):
                other = recv_ref[(g * parts + part) * bands + b].astype(F32)
                tile = tile + other
            for r in range(pairs):
                arrived[b * pairs + r, g * members : (g + 1) * members] = tile[r * members : (r + 1) * members]
        first = recv_ref[b].astype(F32)
        for r in range(pairs):
            row = pairs * members + r
            slots[b * pairs + r] = jnp.broadcast_to(first[row : row + 1], slots.shape[1:])
    innovation = []
    for n in range(positions):
        vector = jnp.zeros(arrived.shape[1:], F32)
        for k in range(bands * pairs):
            vector = vector + jnp.where(slots[k] == float(n), arrived[k], 0.0)
        innovation.append((observed_ref[n : n + 1] - vector).astype(BF))
    innovation = jnp.concatenate(innovation, axis=1)
    weighted = jnp.dot(innovation, precision_ref[...], preferred_element_type=F32)
    for b in range(bands):
        answers = []
        for r in range(pairs):
            slot = slots[b * pairs + r]
            answer = jnp.zeros(arrived.shape[1:], F32)
            for n in range(positions):
                answer = answer + jnp.where(slot == float(n), weighted[:, n * LANES : (n + 1) * LANES], 0.0)
            answers.append(answer)
        for g in range(groups):
            pieces = [answer[g * members : (g + 1) * members] for answer in answers]
            spare = send_ref.shape[1] - pairs * members
            if spare:
                pieces.append(jnp.zeros((spare, LANES), F32))
            tile = jnp.concatenate(pieces, axis=0).astype(BF)
            for part in range(parts):
                send_ref[(g * parts + part) * bands + b] = tile


def backward_kernel(
    dims, recv_ref, picks_ref, at_pixel_ref, win_ref, wmid_ref, wout_ref, total_ref, pre_one_ref, pre_two_ref,
    out_ref, padded, sums, grad_one, grad_two
):
    times, members, chan, width, owners, pairs, extra = dims
    radius = WIN // 2
    rows = members * chan
    zero_state = jnp.zeros((radius, members, chan, width), BF)
    padded[0:radius] = zero_state
    padded[radius + times :] = zero_state
    sums[0:radius] = jnp.zeros((radius, members, chan, width), F32)
    sums[radius + times :] = jnp.zeros((radius, members, chan, width), F32)

    def scatter(t):
        spread = []
        index = lax.broadcasted_iota(jnp.int32, (chan, LANES), 0).astype(BF)
        for o in range(owners):
            tile = recv_ref[t * owners + o]
            for r in range(pairs):
                at_chan = index == row_of(picks_ref, t, rows, o * pairs + r).astype(BF)
                pieces = []
                for m in range(members):
                    row = r * members + m
                    value = jnp.broadcast_to(tile[row : row + 1], (chan, LANES))
                    pieces.append(jnp.where(at_chan, value, jnp.zeros_like(value)))
                spread.append(jnp.concatenate(pieces, axis=0))
        spread = jnp.concatenate(spread, axis=1)
        guidance = jnp.dot(spread, at_pixel_ref[t], preferred_element_type=F32)
        padded[t + radius] = guidance.astype(BF).reshape(members, chan, width)
        sums[t + radius] = (guidance + total_ref[t]).reshape(members, chan, width)

    def first(s):
        for m in range(members):
            window = padded[pl.ds(s, WIN), m].reshape(WIN * chan, width)
            grad = jnp.dot(wout_ref[...], window, preferred_element_type=F32)
            grad_two[s, m] = (grad * twice_slope_of_half(pre_two_ref[s, m])).astype(BF)

    def second(s):
        for m in range(members):
            grad = jnp.dot(wmid_ref[...], grad_two[s, m], preferred_element_type=F32)
            grad_one[s, m] = (grad * twice_slope_of_half(pre_one_ref[s, m])).astype(BF)

    def third(s):
        for m in range(members):
            blocks = jnp.dot(win_ref[...], grad_one[s, m], preferred_element_type=F32)
            sums[pl.ds(s, WIN), m] += blocks.reshape(WIN, chan, width)

    loop(times, scatter)
    loop(times, first)
    loop(times, second)
    loop(times, third)

    def finish(t):
        out_ref[t] = sums[t + radius].reshape(rows, width).astype(BF)

    loop(times, finish)


def body(noisy_state, w_in, w_mid, w_out, obs_pick, obs_slot, observed, precision):
    current = noisy_state[:, 0]
    all_members, chan, pixels = current.shape
    times = lax.axis_size("tm")
    bands = lax.axis_size("lat")
    owners, pairs, block_rows = obs_pick.shape[2:]
    positions = observed.shape[2] // block_rows
    parts = max(1, times // all_members)
    groups = times // parts
    members = all_members // groups
    width = pixels // parts
    radius = WIN // 2
    rows = members * chan
    hidden = w_mid.shape[0]
    extra = ceil_to(3 * owners * pairs * block_rows // width, 16)
    smem = pl.BlockSpec(memory_space=pltpu.SMEM)
    vmem = pl.BlockSpec(memory_space=pltpu.VMEM)
    hbm = pl.BlockSpec(memory_space=pltpu.HBM)
    chunks = 4 if groups % 4 == 0 else 1
    payload, win, wmid, wmid_turned, wout_turned = pl.pallas_call(
        functools.partial(pack_kernel, (groups, parts, members, chan, width, owners, pairs, extra)),
        out_shape=(
            jax.ShapeDtypeStruct((times, rows + extra, width), BF),
            jax.ShapeDtypeStruct(w_in.shape, BF),
            jax.ShapeDtypeStruct(w_mid.shape, BF),
            jax.ShapeDtypeStruct(w_mid.shape[::-1], BF),
            jax.ShapeDtypeStruct(w_out.shape[::-1], BF),
        ),
        in_specs=[hbm] * 6,
        out_specs=(vmem,) * 5,
        scratch_shapes=[
            pltpu.VMEM(current.shape, F32),
            pltpu.VMEM((owners, pairs, block_rows), jnp.int32),
            pltpu.SMEM((pairs, owners), jnp.int32),
            pltpu.VMEM(w_in.shape[::-1], BF),
            pltpu.VMEM(w_mid.shape, BF),
            pltpu.VMEM(w_out.shape, BF),
            pltpu.SemaphoreType.DMA((chunks,)),
            pltpu.SemaphoreType.DMA((5,)),
        ],
        compiler_params=limit(16),
        name="pack",
    )(*(pltpu.with_memory_space_constraint(x, pltpu.HBM) for x in (current, obs_pick[0, 0], obs_slot[0, 0].T, w_in.T, w_mid, w_out)))
    received = lax.all_to_all(payload, "tm", split_axis=0, concat_axis=0, tiled=True)

    offset = ((lax.axis_index("tm") % parts) * width).astype(jnp.int32).reshape(1)
    dims = (times, members, chan, width, owners, pairs, extra)
    rows_two = ceil_to(members * pairs + pairs, 8)
    inner = (times, members, hidden, width)
    padded_shape = (times + 2 * radius, members, chan, width)
    packed, total, pre_one, pre_two, at_pixel = pl.pallas_call(
        functools.partial(forward_kernel, dims),
        out_shape=(
            jax.ShapeDtypeStruct((times * owners, rows_two, LANES), BF),
            jax.ShapeDtypeStruct((times, rows, width), F32),
            jax.ShapeDtypeStruct(inner, F32),
            jax.ShapeDtypeStruct(inner, F32),
            jax.ShapeDtypeStruct((times, owners * pairs * block_rows, width), BF),
        ),
        in_specs=[smem, vmem, vmem, vmem, vmem],
        out_specs=(vmem,) * 5,
        scratch_shapes=[
            pltpu.VMEM(padded_shape, BF),
            pltpu.VMEM(padded_shape, F32),
            pltpu.VMEM(inner, BF),
            pltpu.VMEM(inner, BF),
        ],
        compiler_params=limit(24),
        name="forward",
    )(offset, received, win, wmid, w_out)
    arrived = lax.all_to_all(packed, ("tm", "lat"), split_axis=0, concat_axis=0, tiled=True)
    rows_three = ceil_to(members * pairs, 2)
    answer = pl.pallas_call(
        functools.partial(owner_kernel, (groups, parts, members, bands, pairs, positions)),
        out_shape=jax.ShapeDtypeStruct((times * bands, rows_three, LANES), BF),
        in_specs=[vmem, vmem, vmem],
        out_specs=vmem,
        scratch_shapes=[
            pltpu.VMEM((bands * pairs, all_members, LANES), F32),
            pltpu.VMEM((bands * pairs, all_members, LANES), F32),
        ],
        compiler_params=limit(16),
        name="owner",
    )(arrived, observed.reshape(positions, block_rows), precision[0, 0])
    returned = lax.all_to_all(answer, ("tm", "lat"), split_axis=0, concat_axis=0, tiled=True)
    change = pl.pallas_call(
        functools.partial(backward_kernel, dims),
        out_shape=jax.ShapeDtypeStruct((times, rows, width), BF),
        in_specs=[vmem] * 9,
        out_specs=vmem,
        scratch_shapes=[
            pltpu.VMEM(padded_shape, BF),
            pltpu.VMEM(padded_shape, F32),
            pltpu.VMEM(inner, BF),
            pltpu.VMEM(inner, BF),
        ],
        compiler_params=limit(24),
        name="backward",
    )(returned, received, at_pixel, w_in.T, wmid_turned, wout_turned, total, pre_one, pre_two)
    back = lax.all_to_all(change, "tm", split_axis=0, concat_axis=0, tiled=True)
    back = back.reshape(groups, parts, members, chan, width).transpose(0, 2, 3, 1, 4)
    updated = current + back.reshape(all_members, chan, pixels).astype(F32)
    return updated[:, None]


def solution(mesh):
    in_specs = (
        P(None, "tm", None, "lat"),
        P(),
        P(),
        P(),
        P("tm", "lat", None, None, None),
        P("tm", "lat", None, None),
        P("tm", "lat", None),
        P("tm", "lat", None, None),
    )
    out_specs = P(None, "tm", None, "lat")
    return jax.shard_map(body, mesh=mesh, in_specs=in_specs, out_specs=out_specs, check_vma=False)
```

```python
import functools

import jax
import jax.numpy as jnp
from jax import lax
from jax.experimental import pallas as pl
from jax.experimental.pallas import tpu as pltpu
from jax.sharding import PartitionSpec as P

WIN = 5
LANES = 128
BF = jnp.bfloat16
F32 = jnp.float32


def limit(mib):
    return pltpu.CompilerParams(vmem_limit_bytes=mib * 2**20)


def ceil_to(value, step):
    return -(-value // step) * step


def silu_of_half(half):
    return half + half * jnp.tanh(half)


def twice_slope_of_half(half):
    bend = jnp.tanh(half)
    return (1.0 + bend) * (1.0 + half * (1.0 - bend))


def loop(count, step):
    if count <= 8:
        for index in range(count):
            step(index)
    else:
        lax.fori_loop(0, count, lambda index, carry: (step(index), carry)[1], 0)


def exchange(pieces):
    size = lax.axis_size("tm")
    if len(pieces) == 1:
        return [lax.all_to_all(pieces[0], "tm", split_axis=0, concat_axis=0, tiled=True)]

    def swap(values, distance):
        return lax.ppermute(values, "tm", [(k, k ^ distance) for k in range(size)])

    arrived = [pieces[0]] + [swap(piece, 2 * s) for s, piece in enumerate(pieces) if s]
    return arrived + [swap(piece, 1) for piece in arrived]


def departures(refs, times):
    if len(refs) == 1:
        return [(t, refs[0], t) for t in range(times)]
    me = lax.axis_index("tm")
    return [(((me // 2) ^ s) * 2 + ((me % 2) ^ k), ref, k) for s, ref in enumerate(refs) for k in range(2)]


def arrivals(refs, times):
    if len(refs) == 1:
        return [(t, refs[0], t) for t in range(times)]
    me = lax.axis_index("tm")
    chips = len(refs) // 2
    return [(((me // 2) ^ s) * 2 + ((me % 2) ^ k), refs[k * chips + s], k) for s in range(chips) for k in range(2)]


def pack_kernel(dims, sends, state_hbm, pick_hbm, slot_hbm, win_turned_hbm, wmid_hbm, wout_hbm, observed_hbm, *refs):
    groups, parts, members, chan, width, owners, pairs, extra = dims
    outs = refs[:sends]
    win_ref, wmid_ref, wmid_turned_ref, wout_turned_ref, win_turned, wout, observed = refs[sends : sends + 7]
    state, pick_vmem, slot_ref, wmid, state_sems, sems = refs[sends + 7 :]
    times = groups * parts
    rows = members * chan
    per_row = width // LANES
    rows_each = owners * pairs // per_row
    targets = departures(outs, times)
    small = []
    pairs_of = (
        (pick_hbm, pick_vmem), (slot_hbm, slot_ref), (win_turned_hbm, win_turned), (wmid_hbm, wmid), (wout_hbm, wout),
        (observed_hbm, observed),
    )
    for index, (source, target) in enumerate(pairs_of):
        small.append(pltpu.make_async_copy(source, target, sems.at[index]))
    small[0].start()
    small[1].start()
    copies = []
    for index, (t, _, _) in enumerate(targets):
        if index % parts == 0:
            span = pl.ds((t // parts) * members, members)
            copies.append(pltpu.make_async_copy(state_hbm.at[span], state.at[index // parts], state_sems.at[index // parts]))
            copies[-1].start()
    for copy in small[2:]:
        copy.start()
    small[0].wait()
    small[1].wait()
    pick = pick_vmem[...].astype(F32)
    channel = jnp.floor((pick + 0.5) * (1.0 / (width * parts)))
    place = pick - channel * (width * parts)
    lines = []
    for values in (channel, place):
        for row in range(rows_each):
            cells = [divmod(row * per_row + k, pairs) for k in range(per_row)]
            lines.append(jnp.concatenate([values[o, r : r + 1] for o, r in cells], axis=1))
    for row in range(rows_each):
        cells = [divmod(row * per_row + k, pairs) for k in range(per_row)]
        lines.append(jnp.concatenate([jnp.full((1, LANES), slot_ref[r, o].astype(F32)) for o, r in cells], axis=1))
    if extra > len(lines):
        lines.append(jnp.zeros((extra - len(lines), width), F32))
    lines = jnp.concatenate(lines, axis=0).astype(BF)
    for _, out, row in targets:
        out[row, rows:] = lines
    for index, (t, out, row) in enumerate(targets):
        if index % parts == 0:
            copies[index // parts].wait()
            block = state[index // parts].astype(BF)
        part = index % parts
        out[row, 0:rows] = block[:, :, part * width : (part + 1) * width].reshape(rows, width)
    for copy in small[2:]:
        copy.wait()
    half = jnp.asarray(0.5, BF)
    win_ref[...] = win_turned[...].T * half
    wmid_ref[...] = wmid[...] * half
    wmid_turned_ref[...] = wmid[...].T * half
    wout_turned_ref[...] = wout[...].T * half


def row_of(ref, time, base, block):
    per_row = ref.shape[2] // LANES
    row = base + block // per_row
    start = (block % per_row) * LANES
    return ref[time, row : row + 1, start : start + LANES].astype(F32)


def forward_kernel(dims, offset_ref, win_ref, wmid_ref, wout_ref, *refs):
    send_ref, total_ref, pre_one_ref, pre_two_ref, at_pixel_ref, lines_ref = refs[-10:-4]
    padded, sums, hidden_one, hidden_two = refs[-4:]
    times, members, chan, width, owners, pairs, extra = dims
    radius = WIN // 2
    rows = members * chan
    rows_each = owners * pairs * LANES // width
    zero_state = jnp.zeros((radius, members, chan, width), BF)
    padded[0:radius] = zero_state
    padded[radius + times :] = zero_state
    for t, ref, row in arrivals(refs[:-10], times):
        padded[t + radius] = ref[row, 0:rows].reshape(members, chan, width)
        lines_ref[t] = ref[row, rows:]
    sums[...] = jnp.zeros_like(sums)

    def first(s):
        for m in range(members):
            window = padded[pl.ds(s, WIN), m].reshape(WIN * chan, width)
            pre_one = jnp.dot(win_ref[...], window, preferred_element_type=F32)
            pre_one_ref[s, m] = pre_one
            hidden_one[s, m] = silu_of_half(pre_one).astype(BF)

    def second(s):
        for m in range(members):
            pre_two = jnp.dot(wmid_ref[...], hidden_one[s, m], preferred_element_type=F32)
            pre_two_ref[s, m] = pre_two
            hidden_two[s, m] = silu_of_half(pre_two).astype(BF)

    def third(s):
        for m in range(members):
            blocks = jnp.dot(wout_ref[...], hidden_two[s, m], preferred_element_type=F32)
            sums[pl.ds(s, WIN), m] += blocks.reshape(WIN, chan, width)

    offset = offset_ref[0]
    eight = 8

    def gather(t):
        field = sums[t + radius]
        total_ref[t] = field.reshape(rows, width)
        state = (padded[t + radius].astype(F32) + field).astype(BF).reshape(rows, width)
        index = (lax.broadcasted_iota(jnp.int32, (width, LANES), 0) + offset).astype(BF)
        for o in range(owners):
            lines = []
            for r in range(pairs):
                place = row_of(lines_ref, t, rows_each, o * pairs + r)
                here = index == place.astype(BF)
                lines.append(jnp.where(here, jnp.ones_like(index), jnp.zeros_like(index)))
            at_pixel = jnp.concatenate(lines, axis=1)
            at_pixel_ref[t, o * pairs * LANES : (o + 1) * pairs * LANES] = at_pixel.T
            found = jnp.dot(state, at_pixel, preferred_element_type=F32)
            pieces = []
            for r in range(pairs):
                channel = row_of(lines_ref, t, 0, o * pairs + r)
                high = jnp.floor(channel * (1.0 / eight))
                at_row = lax.broadcasted_iota(jnp.int32, (eight, LANES), 0).astype(F32) == channel - high * eight
                high = jnp.broadcast_to(high, (eight, LANES))
                span = slice(r * LANES, (r + 1) * LANES)
                picked = [found[m * chan : m * chan + eight, span] for m in range(members)]
                for c in range(1, chan // eight):
                    here = high == float(c)
                    for m in range(members):
                        start = m * chan + c * eight
                        picked[m] = jnp.where(here, found[start : start + eight, span], picked[m])
                for m in range(members):
                    pieces.append(jnp.sum(jnp.where(at_row, picked[m], 0.0), axis=0, keepdims=True))
            for r in range(pairs):
                pieces.append(row_of(lines_ref, t, 2 * rows_each, o * pairs + r))
            spare = send_ref.shape[1] - len(pieces)
            if spare:
                pieces.append(jnp.zeros((spare, LANES), F32))
            send_ref[t * owners + o] = jnp.concatenate(pieces, axis=0).astype(BF)

    loop(times, first)
    loop(times, second)
    loop(times, third)
    loop(times, gather)


def owner_kernel(dims, recv_ref, observed_ref, precision_ref, send_ref, arrived, slots):
    groups, parts, members, bands, pairs, positions = dims
    for b in range(bands):
        for g in range(groups):
            tile = recv_ref[(g * parts) * bands + b].astype(F32)
            for part in range(1, parts):
                other = recv_ref[(g * parts + part) * bands + b].astype(F32)
                tile = tile + other
            for r in range(pairs):
                arrived[b * pairs + r, g * members : (g + 1) * members] = tile[r * members : (r + 1) * members]
        first = recv_ref[b].astype(F32)
        for r in range(pairs):
            row = pairs * members + r
            slots[b * pairs + r] = jnp.broadcast_to(first[row : row + 1], slots.shape[1:])
    innovation = []
    for n in range(positions):
        vector = jnp.zeros(arrived.shape[1:], F32)
        for k in range(bands * pairs):
            vector = vector + jnp.where(slots[k] == float(n), arrived[k], 0.0)
        innovation.append((observed_ref[n : n + 1] - vector).astype(BF))
    innovation = jnp.concatenate(innovation, axis=1)
    weighted = jnp.dot(innovation, precision_ref[...], preferred_element_type=F32)
    for b in range(bands):
        answers = []
        for r in range(pairs):
            slot = slots[b * pairs + r]
            answer = jnp.zeros(arrived.shape[1:], F32)
            for n in range(positions):
                answer = answer + jnp.where(slot == float(n), weighted[:, n * LANES : (n + 1) * LANES], 0.0)
            answers.append(answer)
        for g in range(groups):
            pieces = [answer[g * members : (g + 1) * members] for answer in answers]
            spare = send_ref.shape[1] - pairs * members
            if spare:
                pieces.append(jnp.zeros((spare, LANES), F32))
            tile = jnp.concatenate(pieces, axis=0).astype(BF)
            for part in range(parts):
                send_ref[(g * parts + part) * bands + b] = tile


def backward_kernel(
    dims, recv_ref, lines_ref, at_pixel_ref, win_ref, wmid_ref, wout_ref, total_ref, pre_one_ref, pre_two_ref, *refs
):
    padded, sums, grad_one, grad_two = refs[-4:]
    times, members, chan, width, owners, pairs, extra = dims
    radius = WIN // 2
    rows = members * chan
    zero_state = jnp.zeros((radius, members, chan, width), BF)
    padded[0:radius] = zero_state
    padded[radius + times :] = zero_state
    sums[0:radius] = jnp.zeros((radius, members, chan, width), F32)
    sums[radius + times :] = jnp.zeros((radius, members, chan, width), F32)

    def scatter(t):
        spread = []
        index = lax.broadcasted_iota(jnp.int32, (chan, LANES), 0).astype(BF)
        for o in range(owners):
            tile = recv_ref[t * owners + o]
            for r in range(pairs):
                at_chan = index == row_of(lines_ref, t, 0, o * pairs + r).astype(BF)
                pieces = []
                for m in range(members):
                    row = r * members + m
                    value = jnp.broadcast_to(tile[row : row + 1], (chan, LANES))
                    pieces.append(jnp.where(at_chan, value, jnp.zeros_like(value)))
                spread.append(jnp.concatenate(pieces, axis=0))
        spread = jnp.concatenate(spread, axis=1)
        guidance = jnp.dot(spread, at_pixel_ref[t], preferred_element_type=F32)
        padded[t + radius] = guidance.astype(BF).reshape(members, chan, width)
        sums[t + radius] = (guidance + total_ref[t]).reshape(members, chan, width)

    def first(s):
        for m in range(members):
            window = padded[pl.ds(s, WIN), m].reshape(WIN * chan, width)
            grad = jnp.dot(wout_ref[...], window, preferred_element_type=F32)
            grad_two[s, m] = (grad * twice_slope_of_half(pre_two_ref[s, m])).astype(BF)

    def second(s):
        for m in range(members):
            grad = jnp.dot(wmid_ref[...], grad_two[s, m], preferred_element_type=F32)
            grad_one[s, m] = (grad * twice_slope_of_half(pre_one_ref[s, m])).astype(BF)

    def third(s):
        for m in range(members):
            blocks = jnp.dot(win_ref[...], grad_one[s, m], preferred_element_type=F32)
            sums[pl.ds(s, WIN), m] += blocks.reshape(WIN, chan, width)

    loop(times, scatter)
    loop(times, first)
    loop(times, second)
    loop(times, third)

    for t, ref, row in departures(refs[:-4], times):
        ref[row] = sums[t + radius].reshape(rows, width).astype(BF)


def update_kernel(dims, state_ref, *refs):
    times, parts, members, chan, width = dims
    out_hbm, out, sems = refs[-3:]
    copies = []
    for index, (t, ref, row) in enumerate(arrivals(refs[:-3], times)):
        span = pl.ds((t // parts) * members, members)
        part = index % parts
        change = ref[row].reshape(members, chan, width).astype(F32)
        columns = slice(part * width, (part + 1) * width)
        out[span, :, columns] = state_ref[span, :, columns] + change
        if part == parts - 1:
            copies.append(pltpu.make_async_copy(out.at[span], out_hbm.at[span], sems.at[index // parts]))
            copies[-1].start()
    for copy in copies:
        copy.wait()


def body(noisy_state, w_in, w_mid, w_out, obs_pick, obs_slot, observed, precision):
    current = noisy_state[:, 0]
    all_members, chan, pixels = current.shape
    times = lax.axis_size("tm")
    bands = lax.axis_size("lat")
    owners, pairs, block_rows = obs_pick.shape[2:]
    positions = observed.shape[2] // block_rows
    parts = max(1, times // all_members)
    groups = times // parts
    members = all_members // groups
    width = pixels // parts
    radius = WIN // 2
    rows = members * chan
    hidden = w_mid.shape[0]
    extra = ceil_to(3 * owners * pairs * block_rows // width, 16)
    smem = pl.BlockSpec(memory_space=pltpu.SMEM)
    vmem = pl.BlockSpec(memory_space=pltpu.VMEM)
    hbm = pl.BlockSpec(memory_space=pltpu.HBM)
    sends = times // 2 if parts == 1 and times in (4, 8) else 1
    each = times // sends
    sources = (current, obs_pick[0, 0], obs_slot[0, 0].T, w_in.T, w_mid, w_out, observed.reshape(positions, block_rows))
    *payload, win, wmid, wmid_turned, wout_turned, win_turned, wout, seen = pl.pallas_call(
        functools.partial(pack_kernel, (groups, parts, members, chan, width, owners, pairs, extra), sends),
        out_shape=(
            *(jax.ShapeDtypeStruct((each, rows + extra, width), BF) for _ in range(sends)),
            jax.ShapeDtypeStruct(w_in.shape, BF),
            jax.ShapeDtypeStruct(w_mid.shape, BF),
            jax.ShapeDtypeStruct(w_mid.shape[::-1], BF),
            jax.ShapeDtypeStruct(w_out.shape[::-1], BF),
            jax.ShapeDtypeStruct(w_in.shape[::-1], BF),
            jax.ShapeDtypeStruct(w_out.shape, BF),
            jax.ShapeDtypeStruct((positions, block_rows), F32),
        ),
        in_specs=[hbm] * 7,
        out_specs=(vmem,) * (sends + 7),
        scratch_shapes=[
            pltpu.VMEM((groups, members, chan, pixels), F32),
            pltpu.VMEM((owners, pairs, block_rows), jnp.int32),
            pltpu.SMEM((pairs, owners), jnp.int32),
            pltpu.VMEM(w_mid.shape, BF),
            pltpu.SemaphoreType.DMA((groups,)),
            pltpu.SemaphoreType.DMA((6,)),
        ],
        compiler_params=limit(16),
        name="pack",
    )(*(pltpu.with_memory_space_constraint(x, pltpu.HBM) for x in sources))
    received = exchange(payload)

    offset = ((lax.axis_index("tm") % parts) * width).astype(jnp.int32).reshape(1)
    dims = (times, members, chan, width, owners, pairs, extra)
    rows_two = ceil_to(members * pairs + pairs, 8)
    inner = (times, members, hidden, width)
    padded_shape = (times + 2 * radius, members, chan, width)
    packed, total, pre_one, pre_two, at_pixel, lines = pl.pallas_call(
        functools.partial(forward_kernel, dims),
        out_shape=(
            jax.ShapeDtypeStruct((times * owners, rows_two, LANES), BF),
            jax.ShapeDtypeStruct((times, rows, width), F32),
            jax.ShapeDtypeStruct(inner, F32),
            jax.ShapeDtypeStruct(inner, F32),
            jax.ShapeDtypeStruct((times, owners * pairs * block_rows, width), BF),
            jax.ShapeDtypeStruct((times, extra, width), BF),
        ),
        in_specs=[smem] + [vmem] * (3 + len(received)),
        out_specs=(vmem,) * 6,
        scratch_shapes=[
            pltpu.VMEM(padded_shape, BF),
            pltpu.VMEM(padded_shape, F32),
            pltpu.VMEM(inner, BF),
            pltpu.VMEM(inner, BF),
        ],
        compiler_params=limit(24),
        name="forward",
    )(offset, win, wmid, wout, *received)
    arrived = lax.all_to_all(packed, ("tm", "lat"), split_axis=0, concat_axis=0, tiled=True)
    rows_three = ceil_to(members * pairs, 2)
    answer = pl.pallas_call(
        functools.partial(owner_kernel, (groups, parts, members, bands, pairs, positions)),
        out_shape=jax.ShapeDtypeStruct((times * bands, rows_three, LANES), BF),
        in_specs=[vmem, vmem, vmem],
        out_specs=vmem,
        scratch_shapes=[
            pltpu.VMEM((bands * pairs, all_members, LANES), F32),
            pltpu.VMEM((bands * pairs, all_members, LANES), F32),
        ],
        compiler_params=limit(16),
        name="owner",
    )(arrived, seen, precision[0, 0])
    returned = lax.all_to_all(answer, ("tm", "lat"), split_axis=0, concat_axis=0, tiled=True)
    change = pl.pallas_call(
        functools.partial(backward_kernel, dims),
        out_shape=tuple(jax.ShapeDtypeStruct((each, rows, width), BF) for _ in range(sends)),
        in_specs=[vmem] * 9,
        out_specs=(vmem,) * sends,
        scratch_shapes=[
            pltpu.VMEM(padded_shape, BF),
            pltpu.VMEM(padded_shape, F32),
            pltpu.VMEM(inner, BF),
            pltpu.VMEM(inner, BF),
        ],
        compiler_params=limit(24),
        name="backward",
    )(returned, lines, at_pixel, win_turned, wmid_turned, wout_turned, total, pre_one, pre_two)
    back = exchange(change)
    updated = pl.pallas_call(
        functools.partial(update_kernel, (times, parts, members, chan, width)),
        out_shape=jax.ShapeDtypeStruct(current.shape, F32),
        in_specs=[vmem] * (1 + len(back)),
        out_specs=hbm,
        scratch_shapes=[pltpu.VMEM(current.shape, F32), pltpu.SemaphoreType.DMA((groups,))],
        compiler_params=limit(16),
        name="update",
    )(current, *back)
    return updated[:, None]


def solution(mesh):
    in_specs = (
        P(None, "tm", None, "lat"),
        P(),
        P(),
        P(),
        P("tm", "lat", None, None, None),
        P("tm", "lat", None, None),
        P("tm", "lat", None),
        P("tm", "lat", None, None),
    )
    out_specs = P(None, "tm", None, "lat")
    return jax.shard_map(body, mesh=mesh, in_specs=in_specs, out_specs=out_specs, check_vma=False)
```

```python
import functools

import jax
import jax.numpy as jnp
from jax import lax
from jax.experimental import pallas as pl
from jax.experimental.pallas import tpu as pltpu
from jax.sharding import PartitionSpec as P

WIN = 5
LANES = 128
BF = jnp.bfloat16
F32 = jnp.float32


def limit(mib):
    return pltpu.CompilerParams(vmem_limit_bytes=mib * 2**20)


def ceil_to(value, step):
    return -(-value // step) * step


def silu_of_half(half):
    return half + half * jnp.tanh(half)


def twice_slope_of_half(half):
    bend = jnp.tanh(half)
    return (1.0 + bend) * (1.0 + half * (1.0 - bend))


def loop(count, step):
    if count <= 8:
        for index in range(count):
            step(index)
    else:
        lax.fori_loop(0, count, lambda index, carry: (step(index), carry)[1], 0)


def swap(values, distance):
    return lax.ppermute(values, "tm", [(k, k ^ distance) for k in range(lax.axis_size("tm"))])


def exchange(pieces, shifts):
    if shifts is None:
        return [lax.all_to_all(pieces[0], "tm", split_axis=0, concat_axis=0, tiled=True)]
    arrived = [swap(piece, 2 * s) if s else piece for piece, s in zip(pieces, shifts)]
    return arrived + [swap(piece, 1) for piece in arrived]


def departures(refs, times, shifts):
    if shifts is None:
        return [(t, refs[0], t) for t in range(times)]
    me = lax.axis_index("tm")
    return [(((me // 2) ^ s) * 2 + ((me % 2) ^ k), ref, k) for s, ref in zip(shifts, refs) for k in range(2)]


def arrivals(refs, times, shifts):
    if shifts is None:
        return [(t, refs[0], t) for t in range(times)]
    me = lax.axis_index("tm")
    halves = (refs[: len(shifts)], refs[len(shifts) :])
    return [(((me // 2) ^ s) * 2 + ((me % 2) ^ k), halves[k][i], k) for i, s in enumerate(shifts) for k in range(2)]


def put(ref, row, state, lines):
    rows, extra = state.shape[0], lines.shape[0]
    if len(ref.shape) == 3:
        ref[row, 0:rows] = state
        ref[row, rows:] = lines
    else:
        ref[row * (rows + extra) : row * (rows + extra) + rows] = state
        if row == 0:
            ref[rows : rows + extra] = lines


def take(ref, row, rows, extra):
    if len(ref.shape) == 3:
        return ref[row, 0:rows], ref[row, rows:]
    return ref[row * (rows + extra) : row * (rows + extra) + rows], ref[rows : rows + extra]


def pack_kernel(dims, shifts, state_hbm, pick_hbm, slot_hbm, *refs):
    groups, parts, members, chan, width, owners, pairs, extra = dims
    outs, (lines_ref, state, pick_vmem, slot_ref, state_sems, sems) = refs[:-6], refs[-6:]
    times = groups * parts
    rows = members * chan
    per_row = width // LANES
    rows_each = owners * pairs // per_row
    targets = departures(outs, times, shifts)
    small = [pltpu.make_async_copy(pick_hbm, pick_vmem, sems.at[0]), pltpu.make_async_copy(slot_hbm, slot_ref, sems.at[1])]
    for copy in small:
        copy.start()
    copies = []
    for index, (t, _, _) in enumerate(targets):
        if index % parts == 0:
            span = pl.ds((t // parts) * members, members)
            copies.append(pltpu.make_async_copy(state_hbm.at[span], state.at[index // parts], state_sems.at[index // parts]))
            copies[-1].start()
    for copy in small:
        copy.wait()
    pick = pick_vmem[...].astype(F32)
    channel = jnp.floor((pick + 0.5) * (1.0 / (width * parts)))
    place = pick - channel * (width * parts)
    lines = []
    for values in (channel, place):
        for row in range(rows_each):
            cells = [divmod(row * per_row + k, pairs) for k in range(per_row)]
            lines.append(jnp.concatenate([values[o, r : r + 1] for o, r in cells], axis=1))
    for row in range(rows_each):
        cells = [divmod(row * per_row + k, pairs) for k in range(per_row)]
        lines.append(jnp.concatenate([jnp.full((1, LANES), slot_ref[r, o].astype(F32)) for o, r in cells], axis=1))
    if extra > len(lines):
        lines.append(jnp.zeros((extra - len(lines), width), F32))
    lines = jnp.concatenate(lines, axis=0).astype(BF)
    lines_ref[...] = lines
    for index, (t, out, row) in enumerate(targets):
        if index % parts == 0:
            copies[index // parts].wait()
            block = state[index // parts].astype(BF)
        part = index % parts
        put(out, row, block[:, :, part * width : (part + 1) * width].reshape(rows, width), lines)


def prepare_kernel(dims, shifts, lines_ref, state_hbm, win_turned_hbm, wmid_hbm, wout_hbm, observed_hbm, *refs):
    members, chan = dims
    outs, refs = refs[:-9], refs[-9:]
    state, win_ref, wmid_ref, wmid_turned_ref, wout_turned_ref, win_turned, wout, observed, sems = refs[:9]
    rows = members * chan
    moves = (
        (wmid_hbm, wmid_ref), (win_turned_hbm, win_turned), (wout_hbm, wout), (observed_hbm, observed), (state_hbm, state),
    )
    copies = [pltpu.make_async_copy(source, target, sems.at[index]) for index, (source, target) in enumerate(moves)]
    for copy in copies:
        copy.start()
    for copy in copies[:-1]:
        copy.wait()
    half = jnp.asarray(0.5, BF)
    wmid = wmid_ref[...]
    win_ref[...] = win_turned[...].T * half
    wmid_turned_ref[...] = wmid.T * half
    wout_turned_ref[...] = wout[...].T * half
    wmid_ref[...] = wmid * half
    copies[-1].wait()
    if outs:
        for t, out, row in departures(outs, 0, shifts):
            put(out, row, state[pl.ds(t * members, members)].astype(BF).reshape(rows, -1), lines_ref[...])


def row_of(ref, time, base, block):
    per_row = ref.shape[2] // LANES
    row = base + block // per_row
    start = (block % per_row) * LANES
    return ref[time, row : row + 1, start : start + LANES].astype(F32)


def forward_kernel(dims, shifts, offset_ref, win_ref, wmid_ref, wout_ref, *refs):
    send_ref, total_ref, pre_one_ref, pre_two_ref, at_pixel_ref, lines_ref = refs[-10:-4]
    padded, sums, hidden_one, hidden_two = refs[-4:]
    times, members, chan, width, owners, pairs, extra = dims
    radius = WIN // 2
    rows = members * chan
    rows_each = owners * pairs * LANES // width
    zero_state = jnp.zeros((radius, members, chan, width), BF)
    padded[0:radius] = zero_state
    padded[radius + times :] = zero_state
    for t, ref, row in arrivals(refs[:-10], times, shifts):
        state, lines_ref[t] = take(ref, row, rows, extra)
        padded[t + radius] = state.reshape(members, chan, width)
    sums[...] = jnp.zeros_like(sums)

    def first(s):
        for m in range(members):
            window = padded[pl.ds(s, WIN), m].reshape(WIN * chan, width)
            pre_one = jnp.dot(win_ref[...], window, preferred_element_type=F32)
            pre_one_ref[s, m] = pre_one
            hidden_one[s, m] = silu_of_half(pre_one).astype(BF)

    def second(s):
        for m in range(members):
            pre_two = jnp.dot(wmid_ref[...], hidden_one[s, m], preferred_element_type=F32)
            pre_two_ref[s, m] = pre_two
            hidden_two[s, m] = silu_of_half(pre_two).astype(BF)

    def third(s):
        for m in range(members):
            blocks = jnp.dot(wout_ref[...], hidden_two[s, m], preferred_element_type=F32)
            sums[pl.ds(s, WIN), m] += blocks.reshape(WIN, chan, width)

    offset = offset_ref[0]
    eight = 8

    def gather(t):
        field = sums[t + radius]
        total_ref[t] = field.reshape(rows, width)
        state = (padded[t + radius].astype(F32) + field).astype(BF).reshape(rows, width)
        index = (lax.broadcasted_iota(jnp.int32, (width, LANES), 0) + offset).astype(BF)
        for o in range(owners):
            lines = []
            for r in range(pairs):
                place = row_of(lines_ref, t, rows_each, o * pairs + r)
                here = index == place.astype(BF)
                lines.append(jnp.where(here, jnp.ones_like(index), jnp.zeros_like(index)))
            at_pixel = jnp.concatenate(lines, axis=1)
            at_pixel_ref[t, o * pairs * LANES : (o + 1) * pairs * LANES] = at_pixel.T
            found = jnp.dot(state, at_pixel, preferred_element_type=F32)
            pieces = []
            for r in range(pairs):
                channel = row_of(lines_ref, t, 0, o * pairs + r)
                high = jnp.floor(channel * (1.0 / eight))
                at_row = lax.broadcasted_iota(jnp.int32, (eight, LANES), 0).astype(F32) == channel - high * eight
                high = jnp.broadcast_to(high, (eight, LANES))
                span = slice(r * LANES, (r + 1) * LANES)
                picked = [found[m * chan : m * chan + eight, span] for m in range(members)]
                for c in range(1, chan // eight):
                    here = high == float(c)
                    for m in range(members):
                        start = m * chan + c * eight
                        picked[m] = jnp.where(here, found[start : start + eight, span], picked[m])
                for m in range(members):
                    pieces.append(jnp.sum(jnp.where(at_row, picked[m], 0.0), axis=0, keepdims=True))
            for r in range(pairs):
                pieces.append(row_of(lines_ref, t, 2 * rows_each, o * pairs + r))
            spare = send_ref.shape[1] - len(pieces)
            if spare:
                pieces.append(jnp.zeros((spare, LANES), F32))
            send_ref[t * owners + o] = jnp.concatenate(pieces, axis=0).astype(BF)

    loop(times, first)
    loop(times, second)
    loop(times, third)
    loop(times, gather)


def owner_kernel(dims, recv_ref, observed_ref, precision_ref, send_ref, arrived, slots):
    groups, parts, members, bands, pairs, positions = dims
    for b in range(bands):
        for g in range(groups):
            tile = recv_ref[(g * parts) * bands + b].astype(F32)
            for part in range(1, parts):
                other = recv_ref[(g * parts + part) * bands + b].astype(F32)
                tile = tile + other
            for r in range(pairs):
                arrived[b * pairs + r, g * members : (g + 1) * members] = tile[r * members : (r + 1) * members]
        first = recv_ref[b].astype(F32)
        for r in range(pairs):
            row = pairs * members + r
            slots[b * pairs + r] = jnp.broadcast_to(first[row : row + 1], slots.shape[1:])
    innovation = []
    for n in range(positions):
        vector = jnp.zeros(arrived.shape[1:], F32)
        for k in range(bands * pairs):
            vector = vector + jnp.where(slots[k] == float(n), arrived[k], 0.0)
        innovation.append((observed_ref[n : n + 1] - vector).astype(BF))
    innovation = jnp.concatenate(innovation, axis=1)
    weighted = jnp.dot(innovation, precision_ref[...], preferred_element_type=F32)
    for b in range(bands):
        answers = []
        for r in range(pairs):
            slot = slots[b * pairs + r]
            answer = jnp.zeros(arrived.shape[1:], F32)
            for n in range(positions):
                answer = answer + jnp.where(slot == float(n), weighted[:, n * LANES : (n + 1) * LANES], 0.0)
            answers.append(answer)
        for g in range(groups):
            pieces = [answer[g * members : (g + 1) * members] for answer in answers]
            spare = send_ref.shape[1] - pairs * members
            if spare:
                pieces.append(jnp.zeros((spare, LANES), F32))
            tile = jnp.concatenate(pieces, axis=0).astype(BF)
            for part in range(parts):
                send_ref[(g * parts + part) * bands + b] = tile


def backward_kernel(
    dims, shifts, recv_ref, lines_ref, at_pixel_ref, win_ref, wmid_ref, wout_ref, total_ref, pre_one_ref, pre_two_ref, *refs
):
    padded, sums, grad_one, grad_two = refs[-4:]
    times, members, chan, width, owners, pairs, extra = dims
    radius = WIN // 2
    rows = members * chan
    zero_state = jnp.zeros((radius, members, chan, width), BF)
    padded[0:radius] = zero_state
    padded[radius + times :] = zero_state
    sums[0:radius] = jnp.zeros((radius, members, chan, width), F32)
    sums[radius + times :] = jnp.zeros((radius, members, chan, width), F32)

    def scatter(t):
        spread = []
        index = lax.broadcasted_iota(jnp.int32, (chan, LANES), 0).astype(BF)
        for o in range(owners):
            tile = recv_ref[t * owners + o]
            for r in range(pairs):
                at_chan = index == row_of(lines_ref, t, 0, o * pairs + r).astype(BF)
                pieces = []
                for m in range(members):
                    row = r * members + m
                    value = jnp.broadcast_to(tile[row : row + 1], (chan, LANES))
                    pieces.append(jnp.where(at_chan, value, jnp.zeros_like(value)))
                spread.append(jnp.concatenate(pieces, axis=0))
        spread = jnp.concatenate(spread, axis=1)
        guidance = jnp.dot(spread, at_pixel_ref[t], preferred_element_type=F32)
        padded[t + radius] = guidance.astype(BF).reshape(members, chan, width)
        sums[t + radius] = (guidance + total_ref[t]).reshape(members, chan, width)

    def first(s):
        for m in range(members):
            window = padded[pl.ds(s, WIN), m].reshape(WIN * chan, width)
            grad = jnp.dot(wout_ref[...], window, preferred_element_type=F32)
            grad_two[s, m] = (grad * twice_slope_of_half(pre_two_ref[s, m])).astype(BF)

    def second(s):
        for m in range(members):
            grad = jnp.dot(wmid_ref[...], grad_two[s, m], preferred_element_type=F32)
            grad_one[s, m] = (grad * twice_slope_of_half(pre_one_ref[s, m])).astype(BF)

    def third(s):
        for m in range(members):
            blocks = jnp.dot(win_ref[...], grad_one[s, m], preferred_element_type=F32)
            sums[pl.ds(s, WIN), m] += blocks.reshape(WIN, chan, width)

    loop(times, scatter)
    loop(times, first)
    loop(times, second)
    loop(times, third)

    for t, ref, row in departures(refs[:-4], times, shifts):
        ref[row] = sums[t + radius].reshape(rows, width).astype(BF)


def update_kernel(dims, shifts, state_ref, *refs):
    times, parts, members, chan, width = dims
    out_hbm, out, sems = refs[-3:]
    copies = []
    for index, (t, ref, row) in enumerate(arrivals(refs[:-3], times, shifts)):
        span = pl.ds((t // parts) * members, members)
        part = index % parts
        change = ref[row].reshape(members, chan, width).astype(F32)
        columns = slice(part * width, (part + 1) * width)
        out[span, :, columns] = state_ref[span, :, columns] + change
        if part == parts - 1:
            copies.append(pltpu.make_async_copy(out.at[span], out_hbm.at[span], sems.at[index // parts]))
            copies[-1].start()
    for copy in copies:
        copy.wait()


def update_rest_kernel(dims, shifts, written_hbm, state_ref, *refs):
    update_kernel(dims, shifts, state_ref, *refs)


def body(noisy_state, w_in, w_mid, w_out, obs_pick, obs_slot, observed, precision):
    current = noisy_state[:, 0]
    all_members, chan, pixels = current.shape
    times = lax.axis_size("tm")
    bands = lax.axis_size("lat")
    owners, pairs, block_rows = obs_pick.shape[2:]
    positions = observed.shape[2] // block_rows
    parts = max(1, times // all_members)
    groups = times // parts
    members = all_members // groups
    width = pixels // parts
    radius = WIN // 2
    rows = members * chan
    hidden = w_mid.shape[0]
    extra = ceil_to(3 * owners * pairs * block_rows // width, 16)
    smem = pl.BlockSpec(memory_space=pltpu.SMEM)
    vmem = pl.BlockSpec(memory_space=pltpu.VMEM)
    hbm = pl.BlockSpec(memory_space=pltpu.HBM)
    shifts = range(times // 2) if parts == 1 and times in (4, 8) else None
    sends = len(shifts) if shifts else 1
    each = times // sends
    first = 1 if shifts else 0
    here = lambda *arrays: [pltpu.with_memory_space_constraint(x, pltpu.HBM) for x in arrays]
    piece = jax.ShapeDtypeStruct((2 * rows + extra, width) if shifts else (times, rows + extra, width), BF)
    *payload, lines = pl.pallas_call(
        functools.partial(
            pack_kernel, (groups, parts, members, chan, width, owners, pairs, extra), shifts and shifts[1:]
        ),
        out_shape=(*[piece] * (sends - first), jax.ShapeDtypeStruct((extra, width), BF)),
        in_specs=[hbm] * 3,
        out_specs=(vmem,) * (sends - first + 1),
        scratch_shapes=[
            pltpu.VMEM((groups, members, chan, pixels), F32),
            pltpu.VMEM((owners, pairs, block_rows), jnp.int32),
            pltpu.SMEM((pairs, owners), jnp.int32),
            pltpu.SemaphoreType.DMA((groups,)),
            pltpu.SemaphoreType.DMA((2,)),
        ],
        compiler_params=limit(16),
        name="pack",
    )(*here(current, obs_pick[0, 0], obs_slot[0, 0].T))
    *own, state, win, wmid, wmid_turned, wout_turned, win_turned, wout, seen = pl.pallas_call(
        functools.partial(prepare_kernel, (members, chan), shifts and shifts[:1]),
        out_shape=(
            *[piece] * first,
            jax.ShapeDtypeStruct(current.shape, F32),
            jax.ShapeDtypeStruct(w_in.shape, BF),
            jax.ShapeDtypeStruct(w_mid.shape, BF),
            jax.ShapeDtypeStruct(w_mid.shape[::-1], BF),
            jax.ShapeDtypeStruct(w_out.shape[::-1], BF),
            jax.ShapeDtypeStruct(w_in.shape[::-1], BF),
            jax.ShapeDtypeStruct(w_out.shape, BF),
            jax.ShapeDtypeStruct((positions, block_rows), F32),
        ),
        in_specs=[vmem] + [hbm] * 5,
        out_specs=(vmem,) * (first + 8),
        scratch_shapes=[pltpu.SemaphoreType.DMA((5,))],
        compiler_params=limit(16),
        name="prepare",
    )(lines, *here(current, w_in.T, w_mid, w_out, observed.reshape(positions, block_rows)))
    received = exchange(own + payload, shifts)

    offset = ((lax.axis_index("tm") % parts) * width).astype(jnp.int32).reshape(1)
    dims = (times, members, chan, width, owners, pairs, extra)
    rows_two = ceil_to(members * pairs + pairs, 8)
    inner = (times, members, hidden, width)
    padded_shape = (times + 2 * radius, members, chan, width)
    packed, total, pre_one, pre_two, at_pixel, lines = pl.pallas_call(
        functools.partial(forward_kernel, dims, shifts),
        out_shape=(
            jax.ShapeDtypeStruct((times * owners, rows_two, LANES), BF),
            jax.ShapeDtypeStruct((times, rows, width), F32),
            jax.ShapeDtypeStruct(inner, F32),
            jax.ShapeDtypeStruct(inner, F32),
            jax.ShapeDtypeStruct((times, owners * pairs * block_rows, width), BF),
            jax.ShapeDtypeStruct((times, extra, width), BF),
        ),
        in_specs=[smem] + [vmem] * (3 + len(received)),
        out_specs=(vmem,) * 6,
        scratch_shapes=[
            pltpu.VMEM(padded_shape, BF),
            pltpu.VMEM(padded_shape, F32),
            pltpu.VMEM(inner, BF),
            pltpu.VMEM(inner, BF),
        ],
        compiler_params=limit(24),
        name="forward",
    )(offset, win, wmid, wout, *received)
    arrived = lax.all_to_all(packed, ("tm", "lat"), split_axis=0, concat_axis=0, tiled=True)
    rows_three = ceil_to(members * pairs, 2)
    answer = pl.pallas_call(
        functools.partial(owner_kernel, (groups, parts, members, bands, pairs, positions)),
        out_shape=jax.ShapeDtypeStruct((times * bands, rows_three, LANES), BF),
        in_specs=[vmem, vmem, vmem],
        out_specs=vmem,
        scratch_shapes=[
            pltpu.VMEM((bands * pairs, all_members, LANES), F32),
            pltpu.VMEM((bands * pairs, all_members, LANES), F32),
        ],
        compiler_params=limit(16),
        name="owner",
    )(arrived, seen, precision[0, 0])
    returned = lax.all_to_all(answer, ("tm", "lat"), split_axis=0, concat_axis=0, tiled=True)
    change = pl.pallas_call(
        functools.partial(backward_kernel, dims, shifts),
        out_shape=tuple(jax.ShapeDtypeStruct((each, rows, width), BF) for _ in range(sends)),
        in_specs=[vmem] * 9,
        out_specs=(vmem,) * sends,
        scratch_shapes=[
            pltpu.VMEM(padded_shape, BF),
            pltpu.VMEM(padded_shape, F32),
            pltpu.VMEM(inner, BF),
            pltpu.VMEM(inner, BF),
        ],
        compiler_params=limit(24),
        name="backward",
    )(returned, lines, at_pixel, win_turned, wmid_turned, wout_turned, total, pre_one, pre_two)
    back = exchange(change, shifts)
    early = sends // 2
    mates = back[sends:]
    stages = ((back[:early] + mates[:early], shifts[:early]), (back[early:sends] + mates[early:], shifts[early:])) if shifts else ((back, None),)
    updated = None
    for arrays, part_of in stages:
        kernel = update_kernel if updated is None else update_rest_kernel
        written = [] if updated is None else [updated]
        updated = pl.pallas_call(
            functools.partial(kernel, (times, parts, members, chan, width), part_of),
            out_shape=jax.ShapeDtypeStruct(current.shape, F32),
            in_specs=[hbm] * len(written) + [vmem] * (1 + len(arrays)),
            out_specs=hbm,
            scratch_shapes=[pltpu.VMEM(current.shape, F32), pltpu.SemaphoreType.DMA((groups,))],
            input_output_aliases={0: 0} if written else {},
            compiler_params=limit(16),
            name="update",
        )(*written, state, *arrays)
    return updated[:, None]


def solution(mesh):
    in_specs = (
        P(None, "tm", None, "lat"),
        P(),
        P(),
        P(),
        P("tm", "lat", None, None, None),
        P("tm", "lat", None, None),
        P("tm", "lat", None),
        P("tm", "lat", None, None),
    )
    out_specs = P(None, "tm", None, "lat")
    return jax.shard_map(body, mesh=mesh, in_specs=in_specs, out_specs=out_specs, check_vma=False)
```

```python
import functools

import jax
import jax.numpy as jnp
from jax import lax
from jax.experimental import pallas as pl
from jax.experimental.pallas import tpu as pltpu
from jax.sharding import PartitionSpec as P

WIN = 5
LANES = 128
BF = jnp.bfloat16
F32 = jnp.float32


def limit(mib):
    return pltpu.CompilerParams(vmem_limit_bytes=mib * 2**20)


def ceil_to(value, step):
    return -(-value // step) * step


def silu_of_half(half):
    return half + half * jnp.tanh(half)


def twice_slope_of_half(half):
    bend = jnp.tanh(half)
    return (1.0 + bend) * (1.0 + half * (1.0 - bend))


def loop(count, step):
    if count <= 8:
        for index in range(count):
            step(index)
    else:
        lax.fori_loop(0, count, lambda index, carry: (step(index), carry)[1], 0)


def swap(values, distance):
    return lax.ppermute(values, "tm", [(k, k ^ distance) for k in range(lax.axis_size("tm"))])


def exchange(pieces, shifts):
    if shifts is None:
        return [lax.all_to_all(pieces[0], "tm", split_axis=0, concat_axis=0, tiled=True)]
    arrived = [swap(piece, 2 * s) if s else piece for piece, s in zip(pieces, shifts)]
    return arrived + [swap(piece, 1) for piece in arrived]


def departures(refs, times, shifts):
    if shifts is None:
        return [(t, refs[0], t) for t in range(times)]
    me = lax.axis_index("tm")
    return [(((me // 2) ^ s) * 2 + ((me % 2) ^ k), ref, k) for s, ref in zip(shifts, refs) for k in range(2)]


def arrivals(refs, times, shifts):
    if shifts is None:
        return [(t, refs[0], t) for t in range(times)]
    me = lax.axis_index("tm")
    halves = (refs[: len(shifts)], refs[len(shifts) :])
    return [(((me // 2) ^ s) * 2 + ((me % 2) ^ k), halves[k][i], k) for i, s in enumerate(shifts) for k in range(2)]


def put(ref, row, state, lines):
    rows, extra = state.shape[0], lines.shape[0]
    if len(ref.shape) == 3:
        ref[row, 0:rows] = state
        ref[row, rows:] = lines
    else:
        ref[row * (rows + extra) : row * (rows + extra) + rows] = state
        if row == 0:
            ref[rows : rows + extra] = lines


def take(ref, row, rows, extra):
    if len(ref.shape) == 3:
        return ref[row, 0:rows], ref[row, rows:]
    return ref[row * (rows + extra) : row * (rows + extra) + rows], ref[rows : rows + extra]


def pack_kernel(dims, shifts, state_hbm, pick_hbm, slot_hbm, *refs):
    groups, parts, members, chan, width, owners, pairs, extra = dims
    outs, (lines_ref, state, pick_vmem, slot_ref, state_sems, sems) = refs[:-6], refs[-6:]
    times = groups * parts
    rows = members * chan
    per_row = width // LANES
    rows_each = owners * pairs // per_row
    targets = departures(outs, times, shifts)
    small = [pltpu.make_async_copy(pick_hbm, pick_vmem, sems.at[0]), pltpu.make_async_copy(slot_hbm, slot_ref, sems.at[1])]
    for copy in small:
        copy.start()
    copies = []
    for index, (t, _, _) in enumerate(targets):
        if index % parts == 0:
            span = pl.ds((t // parts) * members, members)
            copies.append(pltpu.make_async_copy(state_hbm.at[span], state.at[index // parts], state_sems.at[index // parts]))
            copies[-1].start()
    for copy in small:
        copy.wait()
    pick = pick_vmem[...].astype(F32)
    channel = jnp.floor((pick + 0.5) * (1.0 / (width * parts)))
    place = pick - channel * (width * parts)
    lines = []
    for values in (channel, place):
        for row in range(rows_each):
            cells = [divmod(row * per_row + k, pairs) for k in range(per_row)]
            lines.append(jnp.concatenate([values[o, r : r + 1] for o, r in cells], axis=1))
    for row in range(rows_each):
        cells = [divmod(row * per_row + k, pairs) for k in range(per_row)]
        lines.append(jnp.concatenate([jnp.full((1, LANES), slot_ref[r, o].astype(F32)) for o, r in cells], axis=1))
    if extra > len(lines):
        lines.append(jnp.zeros((extra - len(lines), width), F32))
    lines = jnp.concatenate(lines, axis=0).astype(BF)
    lines_ref[...] = lines
    for index, (t, out, row) in enumerate(targets):
        if index % parts == 0:
            copies[index // parts].wait()
            block = state[index // parts].astype(BF)
        part = index % parts
        put(out, row, block[:, :, part * width : (part + 1) * width].reshape(rows, width), lines)


def two_windows(weights, chan):
    spare = jnp.zeros((chan, weights.shape[1]), weights.dtype)
    return jnp.concatenate(
        [jnp.concatenate([weights, spare], axis=0), jnp.concatenate([spare, weights], axis=0)], axis=1
    )


def prepare_kernel(dims, shifts, lines_ref, state_hbm, win_turned_hbm, wmid_hbm, wout_hbm, observed_hbm, *refs_all):
    members, chan = dims
    outs = refs_all[:-10]
    state, win_ref, wmid_ref, wmid_turned_ref, wout_turned_ref, win_turned_ref, wout, observed = refs_all[-10:-2]
    win_turned, sems = refs_all[-2:]
    rows = members * chan
    moves = (
        (wmid_hbm, wmid_ref), (win_turned_hbm, win_turned), (wout_hbm, wout), (observed_hbm, observed), (state_hbm, state),
    )
    copies = [pltpu.make_async_copy(source, target, sems.at[index]) for index, (source, target) in enumerate(moves)]
    for copy in copies:
        copy.start()
    for copy in copies[:-1]:
        copy.wait()
    half = jnp.asarray(0.5, BF)
    wmid = wmid_ref[...]
    win_turned_ref[...] = two_windows(win_turned[...], chan)
    win_ref[...] = win_turned[...].T * half
    wout_turned_ref[...] = two_windows(wout[...], chan).T * half
    wmid_turned_ref[...] = wmid.T * half
    wmid_ref[...] = wmid * half
    copies[-1].wait()
    if outs:
        for t, out, row in departures(outs, 0, shifts):
            put(out, row, state[pl.ds(t * members, members)].astype(BF).reshape(rows, -1), lines_ref[...])


def row_of(ref, time, base, block):
    per_row = ref.shape[2] // LANES
    row = base + block // per_row
    start = (block % per_row) * LANES
    return ref[time, row : row + 1, start : start + LANES].astype(F32)


def forward_kernel(dims, shifts, offset_ref, win_ref, wmid_ref, wout_ref, *refs):
    send_ref, total_ref, pre_one_ref, pre_two_ref, at_pixel_ref, lines_ref = refs[-10:-4]
    padded, sums, hidden_one, hidden_two = refs[-4:]
    times, members, chan, width, owners, pairs, extra = dims
    radius = WIN // 2
    rows = members * chan
    rows_each = owners * pairs * LANES // width
    zero_state = jnp.zeros((radius, members, chan, width), BF)
    padded[0:radius] = zero_state
    padded[radius + times :] = zero_state
    for t, ref, row in arrivals(refs[:-10], times, shifts):
        state, lines_ref[t] = take(ref, row, rows, extra)
        padded[t + radius] = state.reshape(members, chan, width)
    sums[...] = jnp.zeros_like(sums)

    def first(s):
        for m in range(members):
            window = padded[pl.ds(s, WIN), m].reshape(WIN * chan, width)
            pre_one = jnp.dot(win_ref[...], window, preferred_element_type=F32)
            pre_one_ref[s, m] = pre_one
            hidden_one[s, m] = silu_of_half(pre_one).astype(BF)

    def second(s):
        for m in range(members):
            pre_two = jnp.dot(wmid_ref[...], hidden_one[s, m], preferred_element_type=F32)
            pre_two_ref[s, m] = pre_two
            hidden_two[s, m] = silu_of_half(pre_two).astype(BF)

    def third(s):
        for m in range(members):
            blocks = jnp.dot(wout_ref[...], hidden_two[s, m], preferred_element_type=F32)
            sums[pl.ds(s, WIN), m] += blocks.reshape(WIN, chan, width)

    offset = offset_ref[0]
    eight = 8

    def gather(t):
        field = sums[t + radius]
        total_ref[t] = field.reshape(rows, width)
        state = (padded[t + radius].astype(F32) + field).astype(BF).reshape(rows, width)
        index = (lax.broadcasted_iota(jnp.int32, (width, LANES), 0) + offset).astype(BF)
        for o in range(owners):
            lines = []
            for r in range(pairs):
                place = row_of(lines_ref, t, rows_each, o * pairs + r)
                here = index == place.astype(BF)
                lines.append(jnp.where(here, jnp.ones_like(index), jnp.zeros_like(index)))
            at_pixel = jnp.concatenate(lines, axis=1)
            at_pixel_ref[t, o * pairs * LANES : (o + 1) * pairs * LANES] = at_pixel.T
            found = jnp.dot(state, at_pixel, preferred_element_type=F32)
            pieces = []
            for r in range(pairs):
                channel = row_of(lines_ref, t, 0, o * pairs + r)
                high = jnp.floor(channel * (1.0 / eight))
                at_row = lax.broadcasted_iota(jnp.int32, (eight, LANES), 0).astype(F32) == channel - high * eight
                high = jnp.broadcast_to(high, (eight, LANES))
                span = slice(r * LANES, (r + 1) * LANES)
                picked = [found[m * chan : m * chan + eight, span] for m in range(members)]
                for c in range(1, chan // eight):
                    here = high == float(c)
                    for m in range(members):
                        start = m * chan + c * eight
                        picked[m] = jnp.where(here, found[start : start + eight, span], picked[m])
                for m in range(members):
                    pieces.append(jnp.sum(jnp.where(at_row, picked[m], 0.0), axis=0, keepdims=True))
            for r in range(pairs):
                pieces.append(row_of(lines_ref, t, 2 * rows_each, o * pairs + r))
            spare = send_ref.shape[1] - len(pieces)
            if spare:
                pieces.append(jnp.zeros((spare, LANES), F32))
            send_ref[t * owners + o] = jnp.concatenate(pieces, axis=0).astype(BF)

    loop(times, first)
    loop(times, second)
    loop(times, third)
    loop(times, gather)


def owner_kernel(dims, recv_ref, observed_ref, precision_ref, send_ref, arrived, slots):
    groups, parts, members, bands, pairs, positions = dims
    for b in range(bands):
        for g in range(groups):
            tile = recv_ref[(g * parts) * bands + b].astype(F32)
            for part in range(1, parts):
                other = recv_ref[(g * parts + part) * bands + b].astype(F32)
                tile = tile + other
            for r in range(pairs):
                arrived[b * pairs + r, g * members : (g + 1) * members] = tile[r * members : (r + 1) * members]
        first = recv_ref[b].astype(F32)
        for r in range(pairs):
            row = pairs * members + r
            slots[b * pairs + r] = jnp.broadcast_to(first[row : row + 1], slots.shape[1:])
    innovation = []
    for n in range(positions):
        vector = jnp.zeros(arrived.shape[1:], F32)
        for k in range(bands * pairs):
            vector = vector + jnp.where(slots[k] == float(n), arrived[k], 0.0)
        innovation.append((observed_ref[n : n + 1] - vector).astype(BF))
    innovation = jnp.concatenate(innovation, axis=1)
    weighted = jnp.dot(innovation, precision_ref[...], preferred_element_type=F32)
    for b in range(bands):
        answers = []
        for r in range(pairs):
            slot = slots[b * pairs + r]
            answer = jnp.zeros(arrived.shape[1:], F32)
            for n in range(positions):
                answer = answer + jnp.where(slot == float(n), weighted[:, n * LANES : (n + 1) * LANES], 0.0)
            answers.append(answer)
        for g in range(groups):
            pieces = [answer[g * members : (g + 1) * members] for answer in answers]
            spare = send_ref.shape[1] - pairs * members
            if spare:
                pieces.append(jnp.zeros((spare, LANES), F32))
            tile = jnp.concatenate(pieces, axis=0).astype(BF)
            for part in range(parts):
                send_ref[(g * parts + part) * bands + b] = tile


def backward_kernel(
    dims, shifts, recv_ref, lines_ref, at_pixel_ref, win_ref, wmid_ref, wout_ref, total_ref, pre_one_ref, pre_two_ref, *refs
):
    padded, sums, grad_one, grad_two = refs[-4:]
    times, members, chan, width, owners, pairs, extra = dims
    radius = WIN // 2
    rows = members * chan
    zero_state = jnp.zeros((radius, members, chan, width), BF)
    padded[0:radius] = zero_state
    padded[radius + times :] = zero_state
    sums[0:radius] = jnp.zeros((radius, members, chan, width), F32)
    sums[radius + times :] = jnp.zeros((radius, members, chan, width), F32)

    def scatter(t):
        spread = []
        index = lax.broadcasted_iota(jnp.int32, (chan, LANES), 0).astype(BF)
        for o in range(owners):
            tile = recv_ref[t * owners + o]
            for r in range(pairs):
                at_chan = index == row_of(lines_ref, t, 0, o * pairs + r).astype(BF)
                pieces = []
                for m in range(members):
                    row = r * members + m
                    value = jnp.broadcast_to(tile[row : row + 1], (chan, LANES))
                    pieces.append(jnp.where(at_chan, value, jnp.zeros_like(value)))
                spread.append(jnp.concatenate(pieces, axis=0))
        spread = jnp.concatenate(spread, axis=1)
        guidance = jnp.dot(spread, at_pixel_ref[t], preferred_element_type=F32)
        padded[t + radius] = guidance.astype(BF).reshape(members, chan, width)
        sums[t + radius] = (guidance + total_ref[t]).reshape(members, chan, width)

    def first(pair):
        s = 2 * pair
        for m in range(members):
            fields = padded[pl.ds(s, WIN + 1), m].reshape((WIN + 1) * chan, width)
            grad = jnp.dot(wout_ref[...], fields, preferred_element_type=F32).reshape(2, -1, width)
            grad_two[pl.ds(s, 2), m] = (grad * twice_slope_of_half(pre_two_ref[pl.ds(s, 2), m])).astype(BF)

    def second(s):
        for m in range(members):
            grad = jnp.dot(wmid_ref[...], grad_two[s, m], preferred_element_type=F32)
            grad_one[s, m] = (grad * twice_slope_of_half(pre_one_ref[s, m])).astype(BF)

    def third(pair):
        s = 2 * pair
        for m in range(members):
            grad = grad_one[pl.ds(s, 2), m].reshape(-1, width)
            blocks = jnp.dot(win_ref[...], grad, preferred_element_type=F32)
            sums[pl.ds(s, WIN + 1), m] += blocks.reshape(WIN + 1, chan, width)

    loop(times, scatter)
    loop(times // 2, first)
    loop(times, second)
    loop(times // 2, third)

    for t, ref, row in departures(refs[:-4], times, shifts):
        ref[row] = sums[t + radius].reshape(rows, width).astype(BF)


def update_kernel(dims, places, state_ref, *refs):
    times, parts, members, chan, width = dims
    out_hbm, out, sems = refs[-3:]
    copies = []
    sources = arrivals(refs[:-3], times, None)
    if places is not None:
        me = lax.axis_index("tm")
        sources = [(((me // 2) ^ s) * 2 + ((me % 2) ^ k), ref, k) for (s, k), ref in zip(places, refs)]
    for index, (t, ref, row) in enumerate(sources):
        span = pl.ds((t // parts) * members, members)
        part = index % parts
        change = ref[row].reshape(members, chan, width).astype(F32)
        columns = slice(part * width, (part + 1) * width)
        out[span, :, columns] = state_ref[span, :, columns] + change
        if part == parts - 1:
            copies.append(pltpu.make_async_copy(out.at[span], out_hbm.at[span], sems.at[index // parts]))
            copies[-1].start()
    for copy in copies:
        copy.wait()


def update_rest_kernel(dims, places, written_hbm, state_ref, *refs):
    update_kernel(dims, places, state_ref, *refs)


def body(noisy_state, w_in, w_mid, w_out, obs_pick, obs_slot, observed, precision):
    current = noisy_state[:, 0]
    all_members, chan, pixels = current.shape
    times = lax.axis_size("tm")
    bands = lax.axis_size("lat")
    owners, pairs, block_rows = obs_pick.shape[2:]
    positions = observed.shape[2] // block_rows
    parts = max(1, times // all_members)
    groups = times // parts
    members = all_members // groups
    width = pixels // parts
    radius = WIN // 2
    rows = members * chan
    hidden = w_mid.shape[0]
    extra = ceil_to(3 * owners * pairs * block_rows // width, 16)
    smem = pl.BlockSpec(memory_space=pltpu.SMEM)
    vmem = pl.BlockSpec(memory_space=pltpu.VMEM)
    hbm = pl.BlockSpec(memory_space=pltpu.HBM)
    shifts = range(times // 2) if parts == 1 and times in (4, 8) else None
    sends = len(shifts) if shifts else 1
    each = times // sends
    first = 1 if shifts else 0
    here = lambda *arrays: [pltpu.with_memory_space_constraint(x, pltpu.HBM) for x in arrays]
    piece = jax.ShapeDtypeStruct((2 * rows + extra, width) if shifts else (times, rows + extra, width), BF)
    *payload, lines = pl.pallas_call(
        functools.partial(
            pack_kernel, (groups, parts, members, chan, width, owners, pairs, extra), shifts and shifts[1:]
        ),
        out_shape=(*[piece] * (sends - first), jax.ShapeDtypeStruct((extra, width), BF)),
        in_specs=[hbm] * 3,
        out_specs=(vmem,) * (sends - first + 1),
        scratch_shapes=[
            pltpu.VMEM((groups, members, chan, pixels), F32),
            pltpu.VMEM((owners, pairs, block_rows), jnp.int32),
            pltpu.SMEM((pairs, owners), jnp.int32),
            pltpu.SemaphoreType.DMA((groups,)),
            pltpu.SemaphoreType.DMA((2,)),
        ],
        compiler_params=limit(16),
        name="pack",
    )(*here(current, obs_pick[0, 0], obs_slot[0, 0].T))
    paired = ((WIN + 1) * chan, 2 * hidden)
    *own, state, win, wmid, wmid_turned, wout_turned, win_turned, wout, seen = pl.pallas_call(
        functools.partial(prepare_kernel, (members, chan), shifts and shifts[:1]),
        out_shape=(
            *[piece] * first,
            jax.ShapeDtypeStruct(current.shape, F32),
            jax.ShapeDtypeStruct(w_in.shape, BF),
            jax.ShapeDtypeStruct(w_mid.shape, BF),
            jax.ShapeDtypeStruct(w_mid.shape[::-1], BF),
            jax.ShapeDtypeStruct(paired[::-1], BF),
            jax.ShapeDtypeStruct(paired, BF),
            jax.ShapeDtypeStruct(w_out.shape, BF),
            jax.ShapeDtypeStruct((positions, block_rows), F32),
        ),
        in_specs=[vmem] + [hbm] * 5,
        out_specs=(vmem,) * (first + 8),
        scratch_shapes=[
            pltpu.VMEM(w_in.shape[::-1], BF),
            pltpu.SemaphoreType.DMA((5,)),
        ],
        compiler_params=limit(16),
        name="prepare",
    )(lines, *here(current, w_in.T, w_mid, w_out, observed.reshape(positions, block_rows)))
    received = exchange(own + payload, shifts)

    offset = ((lax.axis_index("tm") % parts) * width).astype(jnp.int32).reshape(1)
    dims = (times, members, chan, width, owners, pairs, extra)
    rows_two = ceil_to(members * pairs + pairs, 8)
    inner = (times, members, hidden, width)
    padded_shape = (times + 2 * radius, members, chan, width)
    packed, total, pre_one, pre_two, at_pixel, lines = pl.pallas_call(
        functools.partial(forward_kernel, dims, shifts),
        out_shape=(
            jax.ShapeDtypeStruct((times * owners, rows_two, LANES), BF),
            jax.ShapeDtypeStruct((times, rows, width), F32),
            jax.ShapeDtypeStruct(inner, F32),
            jax.ShapeDtypeStruct(inner, F32),
            jax.ShapeDtypeStruct((times, owners * pairs * block_rows, width), BF),
            jax.ShapeDtypeStruct((times, extra, width), BF),
        ),
        in_specs=[smem] + [vmem] * (3 + len(received)),
        out_specs=(vmem,) * 6,
        scratch_shapes=[
            pltpu.VMEM(padded_shape, BF),
            pltpu.VMEM(padded_shape, F32),
            pltpu.VMEM(inner, BF),
            pltpu.VMEM(inner, BF),
        ],
        compiler_params=limit(24),
        name="forward",
    )(offset, win, wmid, wout, *received)
    arrived = lax.all_to_all(packed, ("tm", "lat"), split_axis=0, concat_axis=0, tiled=True)
    rows_three = ceil_to(members * pairs, 2)
    answer = pl.pallas_call(
        functools.partial(owner_kernel, (groups, parts, members, bands, pairs, positions)),
        out_shape=jax.ShapeDtypeStruct((times * bands, rows_three, LANES), BF),
        in_specs=[vmem, vmem, vmem],
        out_specs=vmem,
        scratch_shapes=[
            pltpu.VMEM((bands * pairs, all_members, LANES), F32),
            pltpu.VMEM((bands * pairs, all_members, LANES), F32),
        ],
        compiler_params=limit(16),
        name="owner",
    )(arrived, seen, precision[0, 0])
    returned = lax.all_to_all(answer, ("tm", "lat"), split_axis=0, concat_axis=0, tiled=True)
    change = pl.pallas_call(
        functools.partial(backward_kernel, dims, shifts),
        out_shape=tuple(jax.ShapeDtypeStruct((each, rows, width), BF) for _ in range(sends)),
        in_specs=[vmem] * 9,
        out_specs=(vmem,) * sends,
        scratch_shapes=[
            pltpu.VMEM(padded_shape, BF),
            pltpu.VMEM(padded_shape, F32),
            pltpu.VMEM(inner, BF),
            pltpu.VMEM(inner, BF),
        ],
        compiler_params=limit(24),
        name="backward",
    )(returned, lines, at_pixel, win_turned, wmid_turned, wout_turned, total, pre_one, pre_two)
    back = exchange(change, shifts)
    stages = ((back, None),)
    if shifts:
        places = [(s, k) for k in range(2) for s in shifts]
        early = sends + sends // 2
        stages = ((back[:early], places[:early]), (back[early:], places[early:]))
    updated = None
    for arrays, part_of in stages:
        kernel = update_kernel if updated is None else update_rest_kernel
        written = [] if updated is None else [updated]
        updated = pl.pallas_call(
            functools.partial(kernel, (times, parts, members, chan, width), part_of),
            out_shape=jax.ShapeDtypeStruct(current.shape, F32),
            in_specs=[hbm] * len(written) + [vmem] * (1 + len(arrays)),
            out_specs=hbm,
            scratch_shapes=[pltpu.VMEM(current.shape, F32), pltpu.SemaphoreType.DMA((groups,))],
            input_output_aliases={0: 0} if written else {},
            compiler_params=limit(16),
            name="update",
        )(*written, state, *arrays)
    return updated[:, None]


def solution(mesh):
    in_specs = (
        P(None, "tm", None, "lat"),
        P(),
        P(),
        P(),
        P("tm", "lat", None, None, None),
        P("tm", "lat", None, None),
        P("tm", "lat", None),
        P("tm", "lat", None, None),
    )
    out_specs = P(None, "tm", None, "lat")
    return jax.shard_map(body, mesh=mesh, in_specs=in_specs, out_specs=out_specs, check_vma=False)
```
